256 devices in a mesh: slab: 64 (over x, z, y_hi), grp: 4 (over y_lo, core).
Axes of the slice: x: 4, y: 4 (y_hi: 2, y_lo: 2; y = y_hi * 2 + y_lo), z: 8, core: 2. Of those that a mesh axis runs over, the one named last changes fastest.
Arguments:
- fine_input: bfloat16 [128, 128, 128, 128], P('slab', 'grp'), may hold values from -6 to 6
- out_grad: bfloat16 [128, 128, 128, 128], P('slab', 'grp')
- pre_norm: bfloat16 [256, 64, 4096], P('slab', None, 'grp')
- act_out: bfloat16 [256, 64, 4096], P('slab', None, 'grp'), as said below
- norm_gain: float32 [256], P('slab'), may hold values from 0.5 to 2
- w_down: bfloat16 [27, 128, 256], replicated, may hold values from -0.109375 to 0.109375
- w_up: bfloat16 [8, 256, 128], replicated, may hold values from -0.375 to 0.375
Outputs:
- grad_input: bfloat16 [128, 128, 128, 128], P('slab', 'grp')
- grad_down: float32 [256, 27, 128], P(('slab', 'grp'))
- grad_gain: float32 [256], P('slab')
- grad_shift: float32 [256], P('slab')
The draws below stay inside these ranges and needn't reach their ends.
Inputs may be any that keep to these rules, and one draw needn't show every extreme that they name: `act_out`: the ReLU's output saved by the forward pass, zero where a unit was off.
All inputs are finite; a program needn't handle non-finite values.
Results may differ from the reference program's by a relative error of at most 0.0095.
Values may be sent and summed in bfloat16 or wider, within the bound.
A program may use at most 64 MiB of HBM per device.

```python
import math
import jax
import jax.numpy as jnp
from jax import lax

C1 = 128
C2 = 256
MZ = 64
MX = 64
MY = 64
NX = 128
NY = 128
NZ = 128


def saved_fields(key):
    noise_key = jax.random.fold_in(key, 11)
    shift_key = jax.random.fold_in(key, 12)
    offset_key = jax.random.fold_in(key, 13)
    scale_key = jax.random.fold_in(key, 14)
    noise_field = jax.random.normal(noise_key, (C2, MX, MY, MZ), jnp.float32)
    shifts = jax.random.uniform(shift_key, (C2, 1, 1, 1), jnp.float32, -0.5, 0.5)
    offsets = jax.random.uniform(offset_key, (C2, 1, 1, 1), jnp.float32, -1.0, 1.0)
    scales = jnp.exp(jax.random.uniform(scale_key, (C2, 1, 1, 1), jnp.float32, math.log(0.5), math.log(5.0)))
    along_x = jnp.arange(MX, dtype=jnp.float32).reshape(1, MX, 1, 1) / (MX - 1)
    along_y = jnp.arange(MY, dtype=jnp.float32).reshape(1, 1, MY, 1) / (MY - 1)
    ramp_field = jnp.exp(math.log(3.0) * (along_x + along_y))
    return (noise_field, shifts, offsets, scales, ramp_field)


def draw_pre_norm(key, part):
    noise_field, shifts, offsets, scales, ramp_field = saved_fields(key)
    values = offsets + scales * ramp_field * noise_field
    return values.reshape(C2, MX, MY * MZ).astype(jnp.bfloat16)


def draw_act_out(key, part):
    noise_field, shifts, offsets, scales, ramp_field = saved_fields(key)
    values = jnp.maximum(noise_field + shifts, 0.0)
    return values.reshape(C2, MX, MY * MZ).astype(jnp.bfloat16)


def draw_out_grad(key, part):
    noise_key = jax.random.fold_in(key, 21)
    means_key = jax.random.fold_in(key, 22)
    noise_field = jax.random.normal(noise_key, (NX, NY, NZ, C1), jnp.float32)
    channel_means = jax.random.uniform(means_key, (1, 1, 1, C1), jnp.float32, -1.0, 1.0)
    along_x = 0.5 + jnp.arange(NX, dtype=jnp.float32).reshape(NX, 1, 1, 1) / (NX - 1)
    along_y = 0.5 + jnp.arange(NY, dtype=jnp.float32).reshape(1, NY, 1, 1) / (NY - 1)
    return (noise_field + channel_means * along_x * along_y).astype(jnp.bfloat16)


def block_scale(own_key, shape, split, least, high):
    def one(position, shards_of):
        steps = jax.random.uniform(jax.random.fold_in(jax.random.fold_in(own_key, 6), position), (shards_of,), jnp.float32, least / len(split), high / len(split))
        return jnp.repeat(jnp.exp(steps), shape[position] // shards_of).reshape((-1,) + (1,) * (len(shape) - position - 1))

    loudness = one(*split[0])
    for cut in split[1:]:
        loudness = loudness * one(*cut)
    return loudness


def gaussian(key, extent, width, reach, shards=(), kind=jnp.bfloat16):
    values = width * jax.random.normal(key, extent, jnp.float32)
    if shards:
        values = values * block_scale(key, extent, shards, -0.22, 0.18)
    return jnp.clip(values, -reach, reach).astype(kind)


def setup_inputs(seed: int = 0) -> dict:
    seeds = jax.random.split(jax.random.key(seed), 8)
    return {
        "fine_input": gaussian(seeds[0], (NX, NY, NZ, C1), 1.0, 6.0, ((0, 64), (1, 4))),
        "out_grad": draw_out_grad(jax.random.fold_in(seeds[7], 71), 0),
        "pre_norm": draw_pre_norm(jax.random.fold_in(seeds[7], 71), 0),
        "act_out": draw_act_out(jax.random.fold_in(seeds[7], 71), 0),
        "norm_gain": jnp.clip(0.5 + 1.5 * jax.random.uniform(seeds[4], (C2,), jnp.float32) ** block_scale(seeds[4], (C2,), ((0, 64),), -0.2, 0.2), 0.5, 2.0),
        "w_down": gaussian(seeds[5], (27, C1, C2), (27 * C1) ** -0.5, 0.109375),
        "w_up": gaussian(seeds[6], (8, C2, C1), C2 ** -0.5, 0.375),
    }


tap_places = ((1, 1), (0, 0), (1, 0))

def reference(fine_input, out_grad, pre_norm, act_out, norm_gain, w_down, w_up):
    cells = MX * MY * MZ
    grad_split = out_grad.reshape(MX, 2, MY, 2, MZ, 2, C1)
    deep_grad = jnp.zeros((cells, C2), jnp.float32)
    for tap_index in range(8):
        pick_x, pick_y, pick_z = (tap_index // 4, tap_index // 2 % 2, tap_index % 2)
        piece = grad_split[:, pick_x, :, pick_y, :, pick_z, :].reshape(cells, C1)
        deep_grad = deep_grad + jnp.dot(piece, w_up[tap_index].T, preferred_element_type=jnp.float32)
    deep_bf = deep_grad.astype(jnp.bfloat16)
    channel_grad = deep_bf.reshape(MX, MY * MZ, C2).transpose(2, 0, 1).astype(jnp.float32)
    values = pre_norm.astype(jnp.float32)
    channel_mean = lax.optimization_barrier(jnp.sum(values, axis=(1, 2))) / cells
    variance = lax.optimization_barrier(jnp.sum(values * values, axis=(1, 2))) / cells - channel_mean * channel_mean
    inv_std = lax.rsqrt(variance + 1e-05)
    normed = (values - channel_mean[:, None, None]) * inv_std[:, None, None]
    masked = jnp.where(act_out > 0, channel_grad, jnp.zeros_like(channel_grad))
    grad_shift = lax.optimization_barrier(jnp.sum(masked, axis=(1, 2))) / cells
    grad_gain = lax.optimization_barrier(jnp.sum(masked * normed, axis=(1, 2))) / cells
    grad_act = ((norm_gain * inv_std)[:, None, None] * (masked - grad_shift[:, None, None] - normed * grad_gain[:, None, None])).astype(jnp.bfloat16)
    extended = jnp.pad(grad_act.reshape(C2, MX, MY, MZ), ((0, 0), (0, 1), (0, 1), (0, 1)))
    fine_split = fine_input.reshape(MX, 2, MY, 2, MZ, 2, C1)
    blocks = {}
    weights = []
    for tap_index in range(27):
        par_x, off_x = tap_places[tap_index // 9]
        par_y, off_y = tap_places[tap_index // 3 % 3]
        par_z, off_z = tap_places[tap_index % 3]
        window = extended[:, off_x:off_x + MX, off_y:off_y + MY, off_z:off_z + MZ].reshape(C2, cells)
        fine_part = fine_split[:, par_x, :, par_y, :, par_z, :].reshape(cells, C1)
        term = jnp.dot(window.T, w_down[tap_index].T, preferred_element_type=jnp.float32)
        parity = (par_x, par_y, par_z)
        if parity in blocks:
            blocks[parity] = blocks[parity] + term
        else:
            blocks[parity] = term
        weights.append(jnp.dot(window, fine_part, preferred_element_type=jnp.float32))
    ordered = [blocks[par_x, par_y, par_z] for par_x in range(2) for par_y in range(2) for par_z in range(2)]
    stacked = jnp.stack(ordered, 0).reshape(2, 2, 2, MX, MY, MZ, C1)
    grad_input = stacked.transpose(3, 0, 4, 1, 5, 2, 6).reshape(2 * MX, 2 * MY, 2 * MZ, C1).astype(jnp.bfloat16)
    grad_down = jnp.stack(weights, 1) * (1.0 / math.sqrt(cells))
    return (grad_input, grad_down, grad_gain, grad_shift)
```

```python
import functools
import math

import jax
import jax.numpy as jnp
from jax import lax
from jax.experimental import pallas as pl
from jax.experimental.pallas import tpu as pltpu
from jax.sharding import PartitionSpec as P

MESH = pl.DeviceIdType.MESH


def place():
    slab = lax.axis_index("slab")
    grp = lax.axis_index("grp")
    return slab // 16, (slab % 2) * 2 + grp // 2, slab // 2 % 8, grp % 2


def device(x, y, z, core):
    return (x * 16 + z * 2 + y // 2, y % 2 * 2 + core)


def remote(src, dst, send, recv, where):
    return pltpu.make_async_remote_copy(
        src_ref=src, dst_ref=dst, send_sem=send, recv_sem=recv, device_id=where, device_id_type=MESH
    )


FIRST = 14


def rs_peers(x, y, z, core):
    peers = [device(x, y, z, 1 - core)]
    peers += [device((x + d) % 4, y, z, core) for d in (1, 2, 3)]
    peers += [device(x, (y + d) % 4, z, core) for d in (1, 2, 3)]
    peers += [device(x, y, (z + d) % 8, core) for d in range(1, 8)]
    return peers


def rs_kernel(scale, q_ref, out_ref, pair_out, pair_in, ax, ax_in, by, by_in, ay, ay_in, bx, bx_in,
              zz, zs, zs_in, send_sem, recv_sem):
    x, y, z, core = place()
    barrier = pltpu.get_barrier_semaphore()
    peers = rs_peers(x, y, z, core)
    for peer in peers:
        pl.semaphore_signal(barrier, inc=1, device_id=peer, device_id_type=MESH)

    def pack(tap, carry):
        pair_out[tap] = q_ref[tap, 1 - core].astype(jnp.bfloat16)
        return carry

    lax.fori_loop(0, 27, pack, 0)
    pl.semaphore_wait(barrier, len(peers))
    pair = remote(pair_out, pair_in, send_sem.at[0], recv_sem.at[0], peers[0])
    pair.start()
    pair.wait()

    def split_first(tap, carry):
        total = q_ref[tap, core] + pair_in[tap].astype(jnp.float32)
        for block in range(4):
            ax[block, tap] = total[:, block].astype(jnp.bfloat16)
        return carry

    def split_last(tap, carry):
        total = q_ref[tap + FIRST, core] + pair_in[tap + FIRST].astype(jnp.float32)
        for block in range(4):
            by[block, tap] = total[block].astype(jnp.bfloat16)
        return carry

    lax.fori_loop(0, FIRST, split_first, 0)
    wave = []
    for d in (1, 2, 3):
        wave.append(remote(ax.at[(x + d) % 4], ax_in.at[d - 1], send_sem.at[d], recv_sem.at[d], peers[d]))
        wave[-1].start()
    lax.fori_loop(0, 27 - FIRST, split_last, 0)
    for d in (1, 2, 3):
        wave.append(remote(by.at[(y + d) % 4], by_in.at[d - 1], send_sem.at[3 + d], recv_sem.at[3 + d], peers[3 + d]))
        wave[-1].start()
    for copy in wave[:3]:
        copy.wait()

    def add_ax(tap, carry):
        total = ax[x, tap].astype(jnp.float32)
        for d in range(3):
            total = total + ax_in[d, tap].astype(jnp.float32)
        for block in range(4):
            ay[block, tap] = total[block]
        return carry

    lax.fori_loop(0, FIRST, add_ax, 0)
    later = []
    for d in (1, 2, 3):
        later.append(remote(ay.at[(y + d) % 4], ay_in.at[d - 1], send_sem.at[6 + d], recv_sem.at[6 + d], peers[3 + d]))
        later[-1].start()
    for copy in wave[3:]:
        copy.wait()

    def add_by(tap, carry):
        total = by[y, tap].astype(jnp.float32)
        for d in range(3):
            total = total + by_in[d, tap].astype(jnp.float32)
        for block in range(4):
            bx[block, tap] = total[block]
        return carry

    lax.fori_loop(0, 27 - FIRST, add_by, 0)
    for d in (1, 2, 3):
        later.append(remote(bx.at[(x + d) % 4], bx_in.at[d - 1], send_sem.at[9 + d], recv_sem.at[9 + d], peers[d]))
        later[-1].start()
    for copy in later:
        copy.wait()
    for tap in range(27):
        if tap < FIRST:
            total = ay[y, tap] + ay_in[0, tap] + ay_in[1, tap] + ay_in[2, tap]
        else:
            t = tap - FIRST
            total = bx[x, t] + bx_in[0, t] + bx_in[1, t] + bx_in[2, t]
        zz[tap * 8 : tap * 8 + 8, :] = total
    for row in range(8):
        zs[row] = zz[pl.ds(row, 27, stride=8), :]
    last = []
    for d in range(1, 8):
        last.append(remote(zs.at[(z + d) % 8], zs_in.at[d - 1], send_sem.at[12 + d], recv_sem.at[12 + d], peers[6 + d]))
        last[-1].start()
    for copy in last:
        copy.wait()
    total = zs[z]
    for d in range(7):
        total = total + zs_in[d]
    out_ref[...] = total * scale


def reduce_scatter(q, scale):
    bf, f32 = jnp.bfloat16, jnp.float32
    rest = 27 - FIRST
    return pl.pallas_call(
        functools.partial(rs_kernel, scale),
        out_shape=jax.ShapeDtypeStruct((27, 128), f32),
        in_specs=[pl.BlockSpec(memory_space=pltpu.VMEM)],
        out_specs=pl.BlockSpec(memory_space=pltpu.VMEM),
        scratch_shapes=[
            pltpu.VMEM((27, 4, 4, 8, 128), bf),
            pltpu.VMEM((27, 4, 4, 8, 128), bf),
            pltpu.VMEM((4, FIRST, 4, 8, 128), bf),
            pltpu.VMEM((3, FIRST, 4, 8, 128), bf),
            pltpu.VMEM((4, rest, 4, 8, 128), bf),
            pltpu.VMEM((3, rest, 4, 8, 128), bf),
            pltpu.VMEM((4, FIRST, 8, 128), f32),
            pltpu.VMEM((3, FIRST, 8, 128), f32),
            pltpu.VMEM((4, rest, 8, 128), f32),
            pltpu.VMEM((3, rest, 8, 128), f32),
            pltpu.VMEM((216, 128), f32),
            pltpu.VMEM((8, 27, 128), f32),
            pltpu.VMEM((7, 27, 128), f32),
            pltpu.SemaphoreType.DMA((20,)),
            pltpu.SemaphoreType.DMA((20,)),
        ],
        compiler_params=pltpu.CompilerParams(collective_id=0, has_side_effects=True),
    )(q)


tap_places = ((1, 1), (0, 0), (1, 0))


def from_behind(shard, axis, by):
    devices = lax.axis_size(axis)
    pairs = [(i, i + by) for i in range(devices) if 0 <= i + by < devices]
    return lax.ppermute(shard, axis, pairs)


def norm_backward(
    values, grad_vals, saved_act, gain_vals, cell_total, reduce_moments, reduce_terms
):
    moment_one, moment_two = reduce_moments(
        jnp.sum(values, axis=(1, 2)), jnp.sum(values * values, axis=(1, 2))
    )
    channel_mean = moment_one / cell_total
    variance = moment_two / cell_total - channel_mean * channel_mean
    inv_std = lax.rsqrt(variance + 1e-05)
    normed = (values - channel_mean[:, None, None]) * inv_std[:, None, None]
    masked = jnp.where(saved_act > 0, grad_vals, jnp.zeros_like(grad_vals))
    total_one, total_two = reduce_terms(
        jnp.sum(masked, axis=(1, 2)), jnp.sum(masked * normed, axis=(1, 2))
    )
    shift_grad = total_one / cell_total
    gain_grad = total_two / cell_total
    grad_act = (
        (gain_vals * inv_std)[:, None, None]
        * (masked - shift_grad[:, None, None] - normed * gain_grad[:, None, None])
    ).astype(jnp.bfloat16)
    return (grad_act, gain_grad, shift_grad)


def local(fine_input, out_grad, pre_norm, act_out, norm_gain, w_down, w_up):
    fine_planes, fine_rows, fine_depth, width_in = fine_input.shape
    plane_count = fine_planes // 2
    row_count = fine_rows // 2
    depth = fine_depth // 2
    width_deep = w_up.shape[1]
    cell_count = plane_count * row_count * depth
    cell_total = pre_norm.shape[1] * pre_norm.shape[2] * lax.axis_size("grp")
    parity_grad = (
        out_grad.reshape(plane_count, 2, row_count, 2, depth, 2, width_in)
        .transpose(1, 3, 5, 0, 2, 4, 6)
        .reshape(8, cell_count, width_in)
    )
    deep_grad = jnp.einsum("poj,pnj->on", w_up, parity_grad, preferred_element_type=jnp.float32)
    deep_shape = (width_deep, plane_count, row_count * depth)
    deep_bf = deep_grad.astype(jnp.bfloat16).reshape(deep_shape)
    channel_grad = lax.all_to_all(deep_bf, "slab", split_axis=0, concat_axis=1, tiled=True)
    grad_channels, grad_gain, grad_shift = norm_backward(
        pre_norm.astype(jnp.float32),
        channel_grad.astype(jnp.float32),
        act_out,
        norm_gain,
        cell_total,
        lambda first_sum, second_sum: lax.psum((first_sum, second_sum), "grp"),
        lambda first_sum, second_sum: lax.psum((first_sum, second_sum), "grp"),
    )
    back_first = lax.all_to_all(grad_channels, "slab", split_axis=1, concat_axis=0, tiled=True)
    upper = from_behind(back_first, "slab", -1)
    with_plane = jnp.concatenate([back_first, upper], axis=1)
    row_data = from_behind(with_plane[:, :, :depth], "grp", -1)
    extended = jnp.concatenate([with_plane, row_data], axis=2)
    positions = lax.broadcasted_iota(jnp.int32, (1, 1, extended.shape[2]), 2) % depth
    tail_zero = jnp.zeros((width_deep, plane_count + 1, 1), jnp.bfloat16)
    shifted = jnp.where(
        positions != depth - 1,
        jnp.concatenate([extended[:, :, 1:], tail_zero], axis=2),
        jnp.zeros_like(extended),
    )
    fine_split = fine_input.reshape(plane_count, 2, row_count, 2, depth, 2, width_in)

    def window(sources, offsets):
        off_x, off_y, off_z = offsets
        source = sources[1] if off_z else sources[0]
        start_yz = off_y * depth
        return source[
            :, off_x : off_x + plane_count, start_yz : start_yz + row_count * depth
        ].reshape(source.shape[0], cell_count)

    tap_list = []
    for tap_index in range(27):
        par_x, off_x = tap_places[tap_index // 9]
        par_y, off_y = tap_places[tap_index // 3 % 3]
        par_z, off_z = tap_places[tap_index % 3]
        tap_list.append((tap_index, (par_x, par_y, par_z), (off_x, off_y, off_z)))
    fine_blocks = {}
    for par_x in range(2):
        for par_y in range(2):
            for par_z in range(2):
                fine_blocks[par_x, par_y, par_z] = fine_split[
                    :, par_x, :, par_y, :, par_z, :
                ].reshape(cell_count, width_in)
    blocks = {}
    for tap_index, parity, offsets in tap_list:
        term = jnp.einsum(
            "on,jo->nj",
            window((extended, shifted), offsets),
            w_down[tap_index],
            preferred_element_type=jnp.float32,
        )
        if parity in blocks:
            blocks[parity] = blocks[parity] + term
        else:
            blocks[parity] = term
    ordered = [
        blocks[par_x, par_y, par_z]
        for par_x in range(2)
        for par_y in range(2)
        for par_z in range(2)
    ]
    stacked = jnp.stack(ordered, 0).reshape(2, 2, 2, plane_count, row_count, depth, width_in)
    grad_input = (
        stacked.transpose(3, 0, 4, 1, 5, 2, 6)
        .reshape(fine_planes, fine_rows, fine_depth, width_in)
        .astype(jnp.bfloat16)
    )
    grad_scale = 1.0 / math.sqrt(cell_total)
    pieces = [
        piece.reshape(4, 8, 2, 2, 2, *piece.shape[1:])
        .transpose(4, 2, 3, 0, 1, 5, 6)
        .reshape(piece.shape)
        for piece in (extended, shifted)
    ]
    rows_out = [
        jnp.dot(window(pieces, offsets), fine_blocks[parity], preferred_element_type=jnp.float32)
        for tap_index, parity, offsets in tap_list
    ]
    grad_down = reduce_scatter(
        jnp.stack(rows_out, 0).reshape(27, 2, 4, 4, 8, width_in), grad_scale
    )[None]
    return (grad_input, grad_down, grad_gain, grad_shift)


def solution(mesh):
    return jax.shard_map(
        local,
        mesh=mesh,
        in_specs=(
            P("slab", "grp", None, None),
            P("slab", "grp", None, None),
            P("slab", None, "grp"),
            P("slab", None, "grp"),
            P("slab"),
            P(),
            P(),
        ),
        out_specs=(
            P("slab", "grp", None, None),
            P(("slab", "grp"), None, None),
            P("slab"),
            P("slab"),
        ),
        check_vma=False,
    )
```

```python
import functools
import math

import jax
import jax.numpy as jnp
from jax import lax
from jax.experimental import pallas as pl
from jax.experimental.pallas import tpu as pltpu
from jax.sharding import PartitionSpec as P

MESH = pl.DeviceIdType.MESH
BF, F32 = jnp.bfloat16, jnp.float32
FIRST = 14
NT = (((1,), (1,)), ((), ()))
REACH = (((1, 0),), ((2, 0), (0, 1)))


def device(x, y, z, core):
    return (x * 16 + z * 2 + y // 2, y % 2 * 2 + core)


def remote(src, dst, send, recv, where):
    return pltpu.make_async_remote_copy(
        src_ref=src, dst_ref=dst, send_sem=send, recv_sem=recv, device_id=where, device_id_type=MESH
    )


def kernel(
    cells, scale,
    fine_hbm, og_hbm, pn_hbm, act_hbm, gain_ref, wd_hbm, wu_hbm,
    gin_hbm, down_ref, stat_ref,
    fine, og, pn, act, wd, wu, rows32, taps_up, deep32, grad8,
    a1_out, a1_in, a2_out, a2_in, h_in, pn32, act32, moment, term,
    fine_edge, f_even, f_odd, g_own, g_next, gt, gts, q, o32, gin,
    pair_out, pair_in, ax, ax_in, by, by_in, ay, ay_in, bx, bx_in, zz, zs, zs_in,
    load, a1_send, a1_recv, a2_send, a2_recv, h_send, h_recv, m_send, m_recv, t_send, t_recv,
    edge_send, edge_recv, rs_send, rs_recv, store,
):
    slab, grp = lax.axis_index("slab"), lax.axis_index("grp")
    x, y, z, core = slab // 16, slab % 2 * 2 + grp // 2, slab // 2 % 8, grp % 2
    loads = [
        pltpu.make_async_copy(src, dst, load.at[i])
        for i, (src, dst) in enumerate(
            ((og_hbm, og), (wu_hbm, wu), (fine_hbm, fine), (pn_hbm, pn), (act_hbm, act), (wd_hbm, wd))
        )
    ]
    for copy in loads:
        copy.start()
    barrier = pltpu.get_barrier_semaphore()

    def greet(d, carry):
        pl.semaphore_signal(barrier, inc=1, device_id=((slab + d) % 64, grp), device_id_type=MESH)
        return carry

    lax.fori_loop(1, 64, greet, 0)
    for d in (1, 2, 3):
        pl.semaphore_signal(barrier, inc=1, device_id=(slab, (grp + d) % 4), device_id_type=MESH)
    cross = (slab + 1 - slab % 2 * 2, (grp + 2) % 4)
    pl.semaphore_signal(barrier, inc=1, device_id=cross, device_id_type=MESH)

    low = lax.broadcasted_iota(jnp.int32, (8, 512), 0) < 4

    loads[0].wait()
    loads[1].wait()
    for side in range(4):
        taps_up[side] = jnp.concatenate([wu[2 * side], wu[2 * side + 1]], axis=1)

    def part(row, carry):
        for side in range(4):
            rows32[side] = og[side // 2, 2 * row + side % 2].astype(F32)
            at = pl.ds(pl.multiple_of(row * 64, 64), 64)
            grad8[side, at, 0:128] = rows32[side, pl.ds(0, 64, stride=2), :].astype(BF)
            grad8[side, at, 128:256] = rows32[side, pl.ds(1, 64, stride=2), :].astype(BF)
        return carry

    lax.fori_loop(0, 16, part, 0)
    total = lax.dot_general(taps_up[0], grad8[0], NT, preferred_element_type=F32)
    for side in range(1, 4):
        total = total + lax.dot_general(taps_up[side], grad8[side], NT, preferred_element_type=F32)
    deep32[...] = total

    def pieces_of(m, carry):
        at = pl.ds(pl.multiple_of(m * 8, 8), 8)
        left, right = deep32[at, 0:512], deep32[at, 512:1024]
        a1_out[2 * m] = jnp.where(low, left, pltpu.roll(right, 4, 0)).astype(BF)
        a1_out[2 * m + 1] = jnp.where(low, pltpu.roll(left, 4, 0), right).astype(BF)
        return carry

    lax.fori_loop(0, 32, pieces_of, 0)
    pl.semaphore_wait(barrier, 67)

    def a1_copy(d):
        to = (slab + d) % 64
        return remote(a1_out.at[to], a1_in.at[slab], a1_send.at[d], a1_recv.at[d], (to, grp))

    def a1_start(d, carry):
        a1_copy(d).start()
        return carry

    lax.fori_loop(1, 64, a1_start, 0)
    a1_in[slab] = a1_out[slab]

    loads[2].wait()
    edge = remote(fine.at[:, 31], fine_edge, edge_send.at[0], edge_recv.at[0], (slab, (grp + 1) % 4))
    edge.start()
    loads[3].wait()
    loads[4].wait()
    for ch in range(4):
        for half in range(2):
            for block in range(4):
                lanes = slice(half * 512 + block * 128, half * 512 + block * 128 + 128)
                pn32[block, pl.ds(half * 4 + ch, 64, stride=8), :] = pn[ch, :, lanes].astype(F32)
                act32[block, pl.ds(half * 4 + ch, 64, stride=8), :] = act[ch, :, lanes].astype(F32)

    def wide(ref, i):
        at = pl.ds(pl.multiple_of(i * 8, 8), 8)
        return jnp.concatenate([ref[block, at, :] for block in range(4)], axis=1)

    def spread(rows):
        per_row = jnp.sum(rows, axis=1, keepdims=True)
        per_row = jnp.broadcast_to(per_row, (8, 128))
        return per_row + pltpu.roll(per_row, 4, 0)

    def moments(i, carry):
        value = wide(pn32, i)
        return carry[0] + value, carry[1] + value * value

    none = jnp.zeros((8, 512), F32)
    one, two = lax.fori_loop(0, 64, moments, (none, none))
    moment[grp, 0] = spread(one)
    moment[grp, 1] = spread(two)
    m_copies = []
    for d in (1, 2, 3):
        m_copies.append(remote(moment.at[grp], moment.at[grp], m_send.at[d], m_recv.at[d], (slab, (grp + d) % 4)))
        m_copies[-1].start()

    first_row = lax.broadcasted_iota(jnp.int32, (64, 128), 0) == 0

    def place_row(slot, block, values, at):
        rows32[slot] = values.astype(F32)
        even = rows32[slot, pl.ds(0, 64, stride=2), :]
        odd = rows32[slot, pl.ds(1, 64, stride=2), :]
        block[at, 0:128] = jnp.where(first_row, 0.0, pltpu.roll(odd, 1, 0)).astype(BF)
        block[at, 128:256] = even.astype(BF)
        block[at, 256:384] = odd.astype(BF)

    def split_fine(row, carry):
        for plane in range(2):
            place_row(2 * plane, f_even.at[plane], fine[plane, 2 * row], pl.ds(pl.multiple_of(row * 64, 64), 64))
            place_row(
                2 * plane + 1, f_odd.at[plane], fine[plane, 2 * row + 1],
                pl.ds(pl.multiple_of(row * 64 + 64, 64), 64),
            )
        return carry

    lax.fori_loop(0, 16, split_fine, 0)
    edge.wait()
    for plane in range(2):
        behind = fine_edge[plane].astype(F32)
        place_row(plane, f_odd.at[plane], jnp.where(grp == 0, jnp.zeros_like(behind), behind), pl.ds(0, 64))
    for copy in m_copies:
        copy.wait()
    sums = moment[0] + moment[1] + moment[2] + moment[3]
    mean = sums[0] / cells
    inv_std = lax.rsqrt(sums[1] / cells - mean * mean + 1e-05)
    mean_w, inv_w = jnp.tile(mean, (1, 4)), jnp.tile(inv_std, (1, 4))

    def a1_wait(d, carry):
        a1_copy(d).wait()
        return carry

    lax.fori_loop(1, 64, a1_wait, 0)

    def masked_of(i):
        normed = (wide(pn32, i) - mean_w) * inv_w
        masked = jnp.where(wide(act32, i) > 0, a1_in[i].astype(F32), 0.0)
        return masked, normed

    def terms(i, carry):
        masked, normed = masked_of(i)
        return carry[0] + masked, carry[1] + masked * normed

    one, two = lax.fori_loop(0, 64, terms, (none, none))
    term[grp, 0] = spread(one)
    term[grp, 1] = spread(two)
    t_copies = []
    for d in (1, 2, 3):
        t_copies.append(remote(term.at[grp], term.at[grp], t_send.at[d], t_recv.at[d], (slab, (grp + d) % 4)))
        t_copies[-1].start()
    for copy in t_copies:
        copy.wait()
    sums = term[0] + term[1] + term[2] + term[3]
    shift, gain = sums[0] / cells, sums[1] / cells
    stat_ref[0] = gain
    stat_ref[1] = shift
    shift_w, gain_w = jnp.tile(shift, (1, 4)), jnp.tile(gain, (1, 4))
    factor_w = jnp.tile(gain_ref[...] * inv_std, (1, 4))

    def act_grad(i, carry):
        masked, normed = masked_of(i)
        a2_out[i] = (factor_w * (masked - shift_w - normed * gain_w)).astype(BF)
        return carry

    lax.fori_loop(0, 64, act_grad, 0)

    def a2_copy(d):
        to = (slab + d) % 64
        return remote(a2_out.at[to], a2_in.at[slab], a2_send.at[d], a2_recv.at[d], (to, grp))

    def a2_start(d, carry):
        a2_copy(d).start()
        return carry

    lax.fori_loop(1, 64, a2_start, 0)
    a2_in[slab] = a2_out[slab]

    def on_copy(d):
        source = (slab + 64 - d) % 64
        return remote(
            a2_in.at[source], h_in.at[source], h_send.at[d], h_recv.at[d], ((slab + 63) % 64, grp)
        )

    def a2_wait(d, carry):
        a2_copy(d).wait()
        on_copy(d).start()
        return carry

    on_copy(0).start()
    loads[5].wait()
    lax.fori_loop(1, 64, a2_wait, 0)

    def join(source, block):
        def pair_of(m):
            a, b = source[2 * m].astype(F32), source[2 * m + 1].astype(F32)
            left = jnp.where(low, a, pltpu.roll(b, 4, 0))
            right = jnp.where(low, pltpu.roll(a, 4, 0), b)
            return jnp.concatenate([left, right], axis=1)

        def step(m, carry):
            at = pl.ds(pl.multiple_of(m * 16, 16), 16)
            block[at, :] = jnp.concatenate([pair_of(2 * m), pair_of(2 * m + 1)], axis=0).astype(BF)
            return carry

        lax.fori_loop(0, 16, step, 0)

    def tap_grads(kx, block, plane):
        for ky in range(3):
            window = f_even[plane] if ky == 1 else f_odd[plane, ky * 32 : ky * 32 + 1024]
            found = jnp.dot(block[...], window, preferred_element_type=F32)
            for kz in range(3):
                q[9 * kx + 3 * ky + kz] = found[:, kz * 128 : kz * 128 + 128]

    last_cell = lax.broadcasted_iota(jnp.int32, (128, 256), 0) % 64 == 63
    last_row = lax.broadcasted_iota(jnp.int32, (64, 256), 0) == 63

    def turn(block, plane):
        for part in range(8):
            turned = jnp.transpose(block[:, part * 128 : part * 128 + 128].astype(F32))
            gt[plane, part * 128 : part * 128 + 128] = turned.astype(BF)
            moved = jnp.where(last_cell, 0.0, pltpu.roll(turned, 127, 0))
            gts[plane, part * 128 : part * 128 + 128] = moved.astype(BF)

    def edge_row(plane):
        return remote(
            gt.at[plane, 0:64], gt.at[plane, 1024:1088], edge_send.at[1 + plane], edge_recv.at[1 + plane],
            (slab, (grp + 3) % 4),
        )

    def finish_edge(plane):
        edge_row(plane).wait()
        after = gt[plane, 1024:1088].astype(F32)
        after = jnp.where(grp == 3, jnp.zeros_like(after), after)
        gt[plane, 1024:1088] = after.astype(BF)
        gts[plane, 1024:1088] = jnp.where(last_row, 0.0, pltpu.roll(after, 63, 0)).astype(BF)

    def input_grad(px, py):
        def chunk(c, carry):
            both = jnp.zeros((256, 256), F32)
            odd = jnp.zeros((256, 128), F32)
            for kx, off_x in REACH[px]:
                for ky, off_y in REACH[py]:
                    at = pl.ds(pl.multiple_of(c * 256 + off_y * 64, 64), 256)
                    tap = 9 * kx + 3 * ky
                    pair = wd[tap + 1 : tap + 3].reshape(256, 256)
                    both = both + lax.dot_general(gt[off_x, at], pair, NT, preferred_element_type=F32)
                    odd = odd + lax.dot_general(gts[off_x, at], wd[tap], NT, preferred_element_type=F32)
            o32[pl.ds(0, 256, stride=2), :] = both[:, 0:128]
            o32[pl.ds(1, 256, stride=2), :] = both[:, 128:256] + odd
            for row in range(4):
                gin[px, 8 * c + 2 * row + py] = o32[row * 128 : row * 128 + 128].astype(BF)
            return carry

        lax.fori_loop(0, 4, chunk, 0)

    join(a2_in, g_own)
    turn(g_own, 0)
    edge_row(0).start()
    tap_grads(1, g_own, 0)
    tap_grads(2, g_own, 1)
    finish_edge(0)
    input_grad(0, 0)
    input_grad(0, 1)
    gin_copies = [pltpu.make_async_copy(gin.at[px], gin_hbm.at[px], store.at[px]) for px in range(2)]
    gin_copies[0].start()

    def on_wait(d, carry):
        on_copy(d).wait()
        return carry

    lax.fori_loop(0, 64, on_wait, 0)
    join(h_in, g_next)
    ahead = g_next[...].astype(F32)
    g_next[...] = jnp.where(slab == 63, jnp.zeros_like(ahead), ahead).astype(BF)
    tap_grads(0, g_next, 1)

    def pack(tap, carry):
        for side in range(4):
            mine = q[tap, pl.ds(side * 2 + 1 - core, 32, stride=8), :]
            pair_out[tap, side] = mine.astype(BF).reshape(4, 8, 128)
        return carry

    lax.fori_loop(0, 27, pack, 0)
    pair = remote(pair_out, pair_in, rs_send.at[0], rs_recv.at[0], (slab, grp + 1 - 2 * core))
    pair.start()
    turn(g_next, 1)
    edge_row(1).start()
    pair.wait()

    def held(tap, side):
        mine = q[tap, pl.ds(side * 2 + core, 32, stride=8), :].reshape(4, 8, 128)
        return mine + pair_in[tap, side].astype(F32)

    def split_first(tap, carry):
        for side in range(4):
            found = held(tap, side).astype(BF)
            for block in range(4):
                ax[block, tap, side] = found[block]
        return carry

    def split_last(tap, carry):
        for side in range(4):
            by[side, tap] = held(tap + FIRST, side).astype(BF)
        return carry

    lax.fori_loop(0, FIRST, split_first, 0)
    wave, later, last = [], [], []
    for d in (1, 2, 3):
        to = (x + d) % 4
        wave.append(remote(ax.at[to], ax_in.at[d - 1], rs_send.at[d], rs_recv.at[d], device(to, y, z, core)))
        wave[-1].start()
    lax.fori_loop(0, 27 - FIRST, split_last, 0)
    for d in (1, 2, 3):
        to = (y + d) % 4
        wave.append(remote(by.at[to], by_in.at[d - 1], rs_send.at[3 + d], rs_recv.at[3 + d], device(x, to, z, core)))
        wave[-1].start()
    finish_edge(1)
    input_grad(1, 0)
    for copy in wave[:3]:
        copy.wait()

    def add_ax(tap, carry):
        found = ax[x, tap].astype(F32)
        for d in range(3):
            found = found + ax_in[d, tap].astype(F32)
        for block in range(4):
            ay[block, tap] = found[block]
        return carry

    lax.fori_loop(0, FIRST, add_ax, 0)
    for d in (1, 2, 3):
        to = (y + d) % 4
        later.append(remote(ay.at[to], ay_in.at[d - 1], rs_send.at[6 + d], rs_recv.at[6 + d], device(x, to, z, core)))
        later[-1].start()
    for copy in wave[3:]:
        copy.wait()

    def add_by(tap, carry):
        found = by[y, tap].astype(F32)
        for d in range(3):
            found = found + by_in[d, tap].astype(F32)
        for block in range(4):
            bx[block, tap] = found[block]
        return carry

    lax.fori_loop(0, 27 - FIRST, add_by, 0)
    for d in (1, 2, 3):
        to = (x + d) % 4
        later.append(remote(bx.at[to], bx_in.at[d - 1], rs_send.at[9 + d], rs_recv.at[9 + d], device(to, y, z, core)))
        later[-1].start()
    input_grad(1, 1)
    gin_copies[1].start()
    for copy in later:
        copy.wait()
    for tap in range(27):
        if tap < FIRST:
            found = ay[y, tap] + ay_in[0, tap] + ay_in[1, tap] + ay_in[2, tap]
        else:
            t = tap - FIRST
            found = bx[x, t] + bx_in[0, t] + bx_in[1, t] + bx_in[2, t]
        zz[tap * 8 : tap * 8 + 8, :] = found
    for row in range(8):
        zs[row] = zz[pl.ds(row, 27, stride=8), :]
    for d in range(1, 8):
        to = (z + d) % 8
        last.append(remote(zs.at[to], zs_in.at[d - 1], rs_send.at[12 + d], rs_recv.at[12 + d], device(x, y, to, core)))
        last[-1].start()
    for copy in last:
        copy.wait()
    found = zs[z]
    for d in range(7):
        found = found + zs_in[d]
    down_ref[...] = found * scale
    for copy in gin_copies:
        copy.wait()


def local(fine_input, out_grad, pre_norm, act_out, norm_gain, w_down, w_up):
    cells = pre_norm.shape[1] * pre_norm.shape[2] * lax.axis_size("grp")
    gain = jnp.broadcast_to(jnp.tile(norm_gain, 2)[:, None], (8, 128))
    rest = 27 - FIRST
    vmem = pl.BlockSpec(memory_space=pltpu.VMEM)
    anywhere = pl.BlockSpec(memory_space=pl.ANY)
    dma = pltpu.SemaphoreType.DMA
    grad_input, down, stat = pl.pallas_call(
        functools.partial(kernel, float(cells), 1.0 / math.sqrt(cells)),
        out_shape=(
            jax.ShapeDtypeStruct((2, 32, 128, 128), BF),
            jax.ShapeDtypeStruct((27, 128), F32),
            jax.ShapeDtypeStruct((2, 8, 128), F32),
        ),
        in_specs=[anywhere] * 4 + [vmem] + [anywhere] * 2,
        out_specs=(anywhere, vmem, vmem),
        scratch_shapes=[
            pltpu.VMEM((2, 32, 128, 128), BF),
            pltpu.VMEM((2, 32, 128, 128), BF),
            pltpu.VMEM((4, 64, 1024), BF),
            pltpu.VMEM((4, 64, 1024), BF),
            pltpu.VMEM((27, 128, 256), BF),
            pltpu.VMEM((8, 256, 128), BF),
            pltpu.VMEM((4, 128, 128), F32),
            pltpu.VMEM((4, 256, 256), BF),
            pltpu.VMEM((256, 1024), F32),
            pltpu.VMEM((4, 1024, 256), BF),
            pltpu.VMEM((64, 8, 512), BF),
            pltpu.VMEM((64, 8, 512), BF),
            pltpu.VMEM((64, 8, 512), BF),
            pltpu.VMEM((64, 8, 512), BF),
            pltpu.VMEM((64, 8, 512), BF),
            pltpu.VMEM((4, 512, 128), F32),
            pltpu.VMEM((4, 512, 128), F32),
            pltpu.VMEM((4, 2, 8, 128), F32),
            pltpu.VMEM((4, 2, 8, 128), F32),
            pltpu.VMEM((2, 128, 128), BF),
            pltpu.VMEM((2, 1024, 384), BF),
            pltpu.VMEM((2, 1088, 384), BF),
            pltpu.VMEM((256, 1024), BF),
            pltpu.VMEM((256, 1024), BF),
            pltpu.VMEM((2, 1088, 256), BF),
            pltpu.VMEM((2, 1088, 256), BF),
            pltpu.VMEM((27, 256, 128), F32),
            pltpu.VMEM((512, 128), F32),
            pltpu.VMEM((2, 32, 128, 128), BF),
            pltpu.VMEM((27, 4, 4, 8, 128), BF),
            pltpu.VMEM((27, 4, 4, 8, 128), BF),
            pltpu.VMEM((4, FIRST, 4, 8, 128), BF),
            pltpu.VMEM((3, FIRST, 4, 8, 128), BF),
            pltpu.VMEM((4, rest, 4, 8, 128), BF),
            pltpu.VMEM((3, rest, 4, 8, 128), BF),
            pltpu.VMEM((4, FIRST, 8, 128), F32),
            pltpu.VMEM((3, FIRST, 8, 128), F32),
            pltpu.VMEM((4, rest, 8, 128), F32),
            pltpu.VMEM((3, rest, 8, 128), F32),
            pltpu.VMEM((216, 128), F32),
            pltpu.VMEM((8, 27, 128), F32),
            pltpu.VMEM((7, 27, 128), F32),
            dma((6,)),
            dma((64,)), dma((64,)), dma((64,)), dma((64,)), dma((64,)), dma((64,)),
            dma((4,)), dma((4,)), dma((4,)), dma((4,)),
            dma((3,)), dma((3,)), dma((20,)), dma((20,)), dma((2,)),
        ],
        compiler_params=pltpu.CompilerParams(
            collective_id=0, has_side_effects=True, vmem_limit_bytes=60 * 1024 * 1024
        ),
    )(fine_input, out_grad, pre_norm, act_out, gain, w_down, w_up)
    return (grad_input, down[None], stat[0, :4, 0], stat[1, :4, 0])


def solution(mesh):
    return jax.shard_map(
        local,
        mesh=mesh,
        in_specs=(
            P("slab", "grp", None, None),
            P("slab", "grp", None, None),
            P("slab", None, "grp"),
            P("slab", None, "grp"),
            P("slab"),
            P(),
            P(),
        ),
        out_specs=(
            P("slab", "grp", None, None),
            P(("slab", "grp"), None, None),
            P("slab"),
            P("slab"),
        ),
        check_vma=False,
    )
```

```python
import functools
import math

import jax
import jax.numpy as jnp
from jax import lax
from jax.experimental import pallas as pl
from jax.experimental.pallas import tpu as pltpu
from jax.sharding import PartitionSpec as P

MESH = pl.DeviceIdType.MESH
BF, F32 = jnp.bfloat16, jnp.float32
NT = (((1,), (1,)), ((), ()))
REACH = (((1, 0),), ((2, 0), (0, 1)))


def device(x, y, z, core):
    return (x * 16 + z * 2 + y // 2, y % 2 * 2 + core)


def remote(src, dst, send, recv, where):
    return pltpu.make_async_remote_copy(
        src_ref=src, dst_ref=dst, send_sem=send, recv_sem=recv, device_id=where, device_id_type=MESH
    )


def kernel(
    cells, scale,
    fine_hbm, og_hbm, pn_hbm, act_hbm, gain_hbm, wd_hbm, wu_hbm,
    gin, down_ref, stat_ref,
    fine, og, pn, act, wd, wu, gain_ref, rows32, taps_up, deep32, grad8,
    a1_out, a1_in, a2_out, a2_in, h_in, pn32, act32, moment, term,
    fine_edge, f_even, f_odd, g_own, g_next, gt, gts, q, o32,
    pair_out, pair_in, ax, ax_in, by, by_in, ay, ay_in, bx, bx_in, zz, zs, zs_in,
    load, a1_send, a1_recv, a2_send, a2_recv, h_send, h_recv, m_send, m_recv, t_send, t_recv,
    edge_send, edge_recv, rs_send, rs_recv,
):
    slab, grp = lax.axis_index("slab"), lax.axis_index("grp")
    x, y, z, core = slab // 16, slab % 2 * 2 + grp // 2, slab // 2 % 8, grp % 2
    loads = [
        pltpu.make_async_copy(src, dst, load.at[i])
        for i, (src, dst) in enumerate(
            ((og_hbm, og), (wu_hbm, wu), (fine_hbm, fine), (pn_hbm, pn), (act_hbm, act), (wd_hbm, wd), (gain_hbm, gain_ref))
        )
    ]
    for copy in loads:
        copy.start()
    barrier = pltpu.get_barrier_semaphore()

    def greet(d, carry):
        pl.semaphore_signal(barrier, inc=1, device_id=((slab + d) % 64, grp), device_id_type=MESH)
        return carry

    lax.fori_loop(1, 64, greet, 0)
    for d in (1, 2, 3):
        pl.semaphore_signal(barrier, inc=1, device_id=(slab, (grp + d) % 4), device_id_type=MESH)
    cross = (slab + 1 - slab % 2 * 2, (grp + 2) % 4)
    pl.semaphore_signal(barrier, inc=1, device_id=cross, device_id_type=MESH)

    low = lax.broadcasted_iota(jnp.int32, (8, 512), 0) < 4

    loads[0].wait()
    loads[1].wait()
    for side in range(4):
        taps_up[side] = jnp.concatenate([wu[2 * side], wu[2 * side + 1]], axis=1)

    def part(row, carry):
        for side in range(4):
            rows32[side] = og[side // 2, 2 * row + side % 2].astype(F32)
            at = pl.ds(pl.multiple_of(row * 64, 64), 64)
            grad8[side, at, 0:128] = rows32[side, pl.ds(0, 64, stride=2), :].astype(BF)
            grad8[side, at, 128:256] = rows32[side, pl.ds(1, 64, stride=2), :].astype(BF)
        return carry

    lax.fori_loop(0, 16, part, 0)
    total = lax.dot_general(taps_up[0], grad8[0], NT, preferred_element_type=F32)
    for side in range(1, 4):
        total = total + lax.dot_general(taps_up[side], grad8[side], NT, preferred_element_type=F32)
    deep32[...] = total

    def pieces_of(m, carry):
        at = pl.ds(pl.multiple_of(m * 8, 8), 8)
        left, right = deep32[at, 0:512], deep32[at, 512:1024]
        a1_out[2 * m] = jnp.where(low, left, pltpu.roll(right, 4, 0)).astype(BF)
        a1_out[2 * m + 1] = jnp.where(low, pltpu.roll(left, 4, 0), right).astype(BF)
        return carry

    lax.fori_loop(0, 32, pieces_of, 0)
    pl.semaphore_wait(barrier, 67)

    def a1_copy(d):
        to = (slab + d) % 64
        return remote(a1_out.at[to], a1_in.at[slab], a1_send.at[d], a1_recv.at[d], (to, grp))

    def a1_start(d, carry):
        a1_copy(d).start()
        return carry

    lax.fori_loop(1, 64, a1_start, 0)
    a1_in[slab] = a1_out[slab]

    loads[2].wait()
    edge = remote(fine.at[:, 31], fine_edge, edge_send.at[0], edge_recv.at[0], (slab, (grp + 1) % 4))
    edge.start()
    loads[3].wait()
    loads[4].wait()
    loads[6].wait()
    for ch in range(4):
        for half in range(2):
            for block in range(4):
                lanes = slice(half * 512 + block * 128, half * 512 + block * 128 + 128)
                pn32[block, pl.ds(half * 4 + ch, 64, stride=8), :] = pn[ch, :, lanes].astype(F32)
                act32[block, pl.ds(half * 4 + ch, 64, stride=8), :] = act[ch, :, lanes].astype(F32)

    def wide(ref, i):
        at = pl.ds(pl.multiple_of(i * 8, 8), 8)
        return jnp.concatenate([ref[block, at, :] for block in range(4)], axis=1)

    def spread(rows):
        per_row = jnp.sum(rows, axis=1, keepdims=True)
        per_row = jnp.broadcast_to(per_row, (8, 128))
        return per_row + pltpu.roll(per_row, 4, 0)

    def moments(i, carry):
        value = wide(pn32, i)
        return carry[0] + value, carry[1] + value * value

    none = jnp.zeros((8, 512), F32)
    one, two = lax.fori_loop(0, 64, moments, (none, none))
    moment[grp, 0] = spread(one)
    moment[grp, 1] = spread(two)
    m_copies = []
    for d in (1, 2, 3):
        m_copies.append(remote(moment.at[grp], moment.at[grp], m_send.at[d], m_recv.at[d], (slab, (grp + d) % 4)))
        m_copies[-1].start()

    first_row = lax.broadcasted_iota(jnp.int32, (64, 128), 0) == 0

    def place_row(slot, block, values, at):
        rows32[slot] = values.astype(F32)
        even = rows32[slot, pl.ds(0, 64, stride=2), :]
        odd = rows32[slot, pl.ds(1, 64, stride=2), :]
        block[at, 0:128] = jnp.where(first_row, 0.0, pltpu.roll(odd, 1, 0)).astype(BF)
        block[at, 128:256] = even.astype(BF)
        block[at, 256:384] = odd.astype(BF)

    def split_fine(row, carry):
        for plane in range(2):
            place_row(2 * plane, f_even.at[plane], fine[plane, 2 * row], pl.ds(pl.multiple_of(row * 64, 64), 64))
            place_row(
                2 * plane + 1, f_odd.at[plane], fine[plane, 2 * row + 1],
                pl.ds(pl.multiple_of(row * 64 + 64, 64), 64),
            )
        return carry

    lax.fori_loop(0, 16, split_fine, 0)
    edge.wait()
    for plane in range(2):
        behind = fine_edge[plane].astype(F32)
        place_row(plane, f_odd.at[plane], jnp.where(grp == 0, jnp.zeros_like(behind), behind), pl.ds(0, 64))
    for copy in m_copies:
        copy.wait()
    sums = moment[0] + moment[1] + moment[2] + moment[3]
    mean = sums[0] / cells
    inv_std = lax.rsqrt(sums[1] / cells - mean * mean + 1e-05)
    mean_w, inv_w = jnp.tile(mean, (1, 4)), jnp.tile(inv_std, (1, 4))

    def masked_of(i):
        normed = (wide(pn32, i) - mean_w) * inv_w
        masked = jnp.where(wide(act32, i) > 0, a1_in[i].astype(F32), 0.0)
        return masked, normed

    def terms(i, carry):
        masked, normed = masked_of(i)
        return carry[0] + masked, carry[1] + masked * normed

    def a1_wait(d, carry):
        a1_copy(d).wait()
        return terms((slab + 64 - d) % 64, carry)

    one, two = lax.fori_loop(1, 64, a1_wait, terms(slab, (none, none)))
    term[grp, 0] = spread(one)
    term[grp, 1] = spread(two)
    t_copies = []
    for d in (1, 2, 3):
        t_copies.append(remote(term.at[grp], term.at[grp], t_send.at[d], t_recv.at[d], (slab, (grp + d) % 4)))
        t_copies[-1].start()
    for copy in t_copies:
        copy.wait()
    sums = term[0] + term[1] + term[2] + term[3]
    shift, gain = sums[0] / cells, sums[1] / cells
    stat_ref[0] = gain
    stat_ref[1] = shift
    shift_w, gain_w = jnp.tile(shift, (1, 4)), jnp.tile(gain, (1, 4))
    channel = lax.broadcasted_iota(jnp.int32, (8, 128), 0) % 4
    norm_gain = jnp.full((8, 128), gain_ref[0], F32)
    for ch in range(1, 4):
        norm_gain = jnp.where(channel == ch, gain_ref[ch], norm_gain)
    factor_w = jnp.tile(norm_gain * inv_std, (1, 4))

    def act_grad(i):
        masked, normed = masked_of(i)
        a2_out[i] = (factor_w * (masked - shift_w - normed * gain_w)).astype(BF)

    def a2_copy(d):
        to = (slab + d) % 64
        return remote(a2_out.at[to], a2_in.at[slab], a2_send.at[d], a2_recv.at[d], (to, grp))

    def a2_start(d, carry):
        act_grad((slab + d) % 64)
        a2_copy(d - 1).start()
        return carry

    act_grad((slab + 1) % 64)
    lax.fori_loop(2, 64, a2_start, 0)
    act_grad(slab)
    a2_copy(63).start()
    a2_in[slab] = a2_out[slab]

    def on_copy(d):
        source = (slab + 64 - d) % 64
        return remote(
            a2_in.at[source], h_in.at[source], h_send.at[d], h_recv.at[d], ((slab + 63) % 64, grp)
        )

    def a2_wait(d, carry):
        a2_copy(d).wait()
        on_copy(d).start()
        return carry

    on_copy(0).start()
    loads[5].wait()
    lax.fori_loop(1, 64, a2_wait, 0)

    def join(source, block):
        def pair_of(m):
            a, b = source[2 * m].astype(F32), source[2 * m + 1].astype(F32)
            left = jnp.where(low, a, pltpu.roll(b, 4, 0))
            right = jnp.where(low, pltpu.roll(a, 4, 0), b)
            return jnp.concatenate([left, right], axis=1)

        def step(m, carry):
            at = pl.ds(pl.multiple_of(m * 16, 16), 16)
            block[at, :] = jnp.concatenate([pair_of(2 * m), pair_of(2 * m + 1)], axis=0).astype(BF)
            return carry

        lax.fori_loop(0, 16, step, 0)

    def tap_grads(kx, block, plane):
        for ky in range(3):
            window = f_even[plane] if ky == 1 else f_odd[plane, ky * 32 : ky * 32 + 1024]
            found = jnp.dot(block[...], window, preferred_element_type=F32)
            for kz in range(3):
                q[9 * kx + 3 * ky + kz] = found[:, kz * 128 : kz * 128 + 128]

    last_cell = lax.broadcasted_iota(jnp.int32, (128, 256), 0) % 64 == 63
    last_row = lax.broadcasted_iota(jnp.int32, (64, 256), 0) == 63

    def turn(block, plane):
        for part in range(8):
            turned = jnp.transpose(block[:, part * 128 : part * 128 + 128].astype(F32))
            gt[plane, part * 128 : part * 128 + 128] = turned.astype(BF)
            moved = jnp.where(last_cell, 0.0, pltpu.roll(turned, 127, 0))
            gts[plane, part * 128 : part * 128 + 128] = moved.astype(BF)

    def edge_row(plane):
        return remote(
            gt.at[plane, 0:64], gt.at[plane, 1024:1088], edge_send.at[1 + plane], edge_recv.at[1 + plane],
            (slab, (grp + 3) % 4),
        )

    def finish_edge(plane):
        edge_row(plane).wait()
        after = gt[plane, 1024:1088].astype(F32)
        after = jnp.where(grp == 3, jnp.zeros_like(after), after)
        gt[plane, 1024:1088] = after.astype(BF)
        gts[plane, 1024:1088] = jnp.where(last_row, 0.0, pltpu.roll(after, 63, 0)).astype(BF)

    def input_grad(px, py, begin=0, end=4):
        def chunk(c, carry):
            both = jnp.zeros((256, 256), F32)
            odd = jnp.zeros((256, 128), F32)
            for kx, off_x in REACH[px]:
                for ky, off_y in REACH[py]:
                    at = pl.ds(pl.multiple_of(c * 256 + off_y * 64, 64), 256)
                    tap = 9 * kx + 3 * ky
                    pair = wd[tap + 1 : tap + 3].reshape(256, 256)
                    both = both + lax.dot_general(gt[off_x, at], pair, NT, preferred_element_type=F32)
                    odd = odd + lax.dot_general(gts[off_x, at], wd[tap], NT, preferred_element_type=F32)
            o32[pl.ds(0, 256, stride=2), :] = both[:, 0:128]
            o32[pl.ds(1, 256, stride=2), :] = both[:, 128:256] + odd
            for row in range(4):
                gin[px, 8 * c + 2 * row + py] = o32[row * 128 : row * 128 + 128].astype(BF)
            return carry

        lax.fori_loop(begin, end, chunk, 0)

    def pack(first, slot):
        def step(i, carry):
            for side in range(4):
                found = q[first + i, pl.ds(side * 2 + 1 - core, 32, stride=8), :]
                pair_out[slot + i, side] = found.astype(BF).reshape(4, 8, 128)
            return carry

        lax.fori_loop(0, 9, step, 0)

    def pair_copy(part):
        at = pl.ds(part * 9, 9)
        return remote(
            pair_out.at[at], pair_in.at[at], rs_send.at[part], rs_recv.at[part], (slab, grp + 1 - 2 * core)
        )

    def held(tap, slot, side):
        found = q[tap, pl.ds(side * 2 + core, 32, stride=8), :].reshape(4, 8, 128)
        return found + pair_in[slot, side].astype(F32)

    def ax_copy(part, d):
        to, i, at = (x + d) % 4, 2 + part * 3 + d, pl.ds(part * 9, 9)
        return remote(ax.at[to, at], ax_in.at[d - 1, at], rs_send.at[i], rs_recv.at[i], device(to, y, z, core))

    def by_copy(d):
        to, i = (y + d) % 4, 8 + d
        return remote(by.at[to], by_in.at[d - 1], rs_send.at[i], rs_recv.at[i], device(x, to, z, core))

    def ay_copy(d):
        to, i = (y + d) % 4, 11 + d
        return remote(ay.at[to], ay_in.at[d - 1], rs_send.at[i], rs_recv.at[i], device(x, to, z, core))

    def bx_copy(d):
        to, i = (x + d) % 4, 14 + d
        return remote(bx.at[to], bx_in.at[d - 1], rs_send.at[i], rs_recv.at[i], device(to, y, z, core))

    def split_x(part):
        def step(i, carry):
            slot = part * 9 + i
            for side in range(4):
                found = held(9 + slot, slot, side).astype(BF)
                for block in range(4):
                    ax[block, slot, side] = found[block]
            return carry

        lax.fori_loop(0, 9, step, 0)

    join(a2_in, g_own)
    tap_grads(1, g_own, 0)
    pack(9, 0)
    pair_copy(0).start()
    tap_grads(2, g_own, 1)
    pack(18, 9)
    pair_copy(1).start()
    turn(g_own, 0)
    edge_row(0).start()
    for part in range(2):
        pair_copy(part).wait()
        split_x(part)
        for d in (1, 2, 3):
            ax_copy(part, d).start()
    finish_edge(0)
    input_grad(0, 0)
    input_grad(0, 1)

    def on_wait(d, carry):
        on_copy(d).wait()
        return carry

    lax.fori_loop(0, 64, on_wait, 0)
    join(h_in, g_next)
    ahead = g_next[...].astype(F32)
    g_next[...] = jnp.where(slab == 63, jnp.zeros_like(ahead), ahead).astype(BF)
    tap_grads(0, g_next, 1)
    pack(0, 18)
    pair_copy(2).start()
    turn(g_next, 1)
    edge_row(1).start()
    pair_copy(2).wait()

    def split_y(i, carry):
        for side in range(4):
            by[side, i] = held(i, 18 + i, side).astype(BF)
        return carry

    lax.fori_loop(0, 9, split_y, 0)
    for d in (1, 2, 3):
        by_copy(d).start()
    for part in range(2):
        for d in (1, 2, 3):
            ax_copy(part, d).wait()

    def add_x(slot, carry):
        found = ax[x, slot].astype(F32)
        for d in range(3):
            found = found + ax_in[d, slot].astype(F32)
        for block in range(4):
            ay[block, slot] = found[block]
        return carry

    lax.fori_loop(0, 18, add_x, 0)
    for d in (1, 2, 3):
        ay_copy(d).start()
    finish_edge(1)
    input_grad(1, 0)
    for d in (1, 2, 3):
        by_copy(d).wait()

    def add_y(i, carry):
        found = by[y, i].astype(F32)
        for d in range(3):
            found = found + by_in[d, i].astype(F32)
        for block in range(4):
            bx[block, i] = found[block]
        return carry

    lax.fori_loop(0, 9, add_y, 0)
    for d in (1, 2, 3):
        bx_copy(d).start()
    input_grad(1, 1, 0, 2)
    for d in (1, 2, 3):
        ay_copy(d).wait()
        bx_copy(d).wait()
    for tap in range(27):
        if tap < 9:
            found = bx[x, tap] + bx_in[0, tap] + bx_in[1, tap] + bx_in[2, tap]
        else:
            t = tap - 9
            found = ay[y, t] + ay_in[0, t] + ay_in[1, t] + ay_in[2, t]
        zz[tap * 8 : tap * 8 + 8, :] = found
    for row in range(8):
        zs[row] = zz[pl.ds(row, 27, stride=8), :]
    def z_copy(d):
        to, i = (z + d) % 8, 17 + d
        return remote(zs.at[to], zs_in.at[d - 1], rs_send.at[i], rs_recv.at[i], device(x, y, to, core))

    for d in range(1, 8):
        z_copy(d).start()
    input_grad(1, 1, 2, 4)
    for d in range(1, 8):
        z_copy(d).wait()
    found = zs[z]
    for d in range(7):
        found = found + zs_in[d]
    for tap in range(27):
        down_ref[tap] = found[tap : tap + 1] * scale


def write(gin, down, stat, gin_out, down_out, gain_out, shift_out, sem):
    copies = [
        pltpu.make_async_copy(gin, gin_out, sem.at[0]),
        pltpu.make_async_copy(down, down_out, sem.at[1]),
    ]
    for copy in copies:
        copy.start()
    row = lax.broadcasted_iota(jnp.int32, (8, 128), 0)
    lane = lax.broadcasted_iota(jnp.int32, (8, 128), 1)
    for ch in range(4):
        here = (row == ch) & (lane == 0)
        gain_out[ch] = jnp.sum(jnp.where(here, stat[0], 0.0))
        shift_out[ch] = jnp.sum(jnp.where(here, stat[1], 0.0))
    for copy in copies:
        copy.wait()


def local(fine_input, out_grad, pre_norm, act_out, norm_gain, w_down, w_up):
    cells = pre_norm.shape[1] * pre_norm.shape[2] * lax.axis_size("grp")
    arrays = (fine_input, out_grad, pre_norm, act_out, norm_gain, w_down, w_up)
    vmem = pl.BlockSpec(memory_space=pltpu.VMEM)
    smem = pl.BlockSpec(memory_space=pltpu.SMEM)
    hbm = pl.BlockSpec(memory_space=pltpu.HBM)
    dma = pltpu.SemaphoreType.DMA
    grad_input, down, stat = pl.pallas_call(
        functools.partial(kernel, float(cells), 1.0 / math.sqrt(cells)),
        out_shape=(
            jax.ShapeDtypeStruct((2, 32, 128, 128), BF),
            jax.ShapeDtypeStruct((27, 1, 128), F32),
            jax.ShapeDtypeStruct((2, 8, 128), F32),
        ),
        in_specs=[hbm] * 7,
        out_specs=(vmem, vmem, vmem),
        scratch_shapes=[
            pltpu.VMEM((2, 32, 128, 128), BF),
            pltpu.VMEM((2, 32, 128, 128), BF),
            pltpu.VMEM((4, 64, 1024), BF),
            pltpu.VMEM((4, 64, 1024), BF),
            pltpu.VMEM((27, 128, 256), BF),
            pltpu.VMEM((8, 256, 128), BF),
            pltpu.SMEM((4,), F32),
            pltpu.VMEM((4, 128, 128), F32),
            pltpu.VMEM((4, 256, 256), BF),
            pltpu.VMEM((256, 1024), F32),
            pltpu.VMEM((4, 1024, 256), BF),
            pltpu.VMEM((64, 8, 512), BF),
            pltpu.VMEM((64, 8, 512), BF),
            pltpu.VMEM((64, 8, 512), BF),
            pltpu.VMEM((64, 8, 512), BF),
            pltpu.VMEM((64, 8, 512), BF),
            pltpu.VMEM((4, 512, 128), F32),
            pltpu.VMEM((4, 512, 128), F32),
            pltpu.VMEM((4, 2, 8, 128), F32),
            pltpu.VMEM((4, 2, 8, 128), F32),
            pltpu.VMEM((2, 128, 128), BF),
            pltpu.VMEM((2, 1024, 384), BF),
            pltpu.VMEM((2, 1088, 384), BF),
            pltpu.VMEM((256, 1024), BF),
            pltpu.VMEM((256, 1024), BF),
            pltpu.VMEM((2, 1088, 256), BF),
            pltpu.VMEM((2, 1088, 256), BF),
            pltpu.VMEM((27, 256, 128), F32),
            pltpu.VMEM((512, 128), F32),
            pltpu.VMEM((27, 4, 4, 8, 128), BF),
            pltpu.VMEM((27, 4, 4, 8, 128), BF),
            pltpu.VMEM((4, 18, 4, 8, 128), BF),
            pltpu.VMEM((3, 18, 4, 8, 128), BF),
            pltpu.VMEM((4, 9, 4, 8, 128), BF),
            pltpu.VMEM((3, 9, 4, 8, 128), BF),
            pltpu.VMEM((4, 18, 8, 128), F32),
            pltpu.VMEM((3, 18, 8, 128), F32),
            pltpu.VMEM((4, 9, 8, 128), F32),
            pltpu.VMEM((3, 9, 8, 128), F32),
            pltpu.VMEM((216, 128), F32),
            pltpu.VMEM((8, 27, 128), F32),
            pltpu.VMEM((7, 27, 128), F32),
            dma((7,)),
            dma((64,)), dma((64,)), dma((64,)), dma((64,)), dma((64,)), dma((64,)),
            dma((4,)), dma((4,)), dma((4,)), dma((4,)),
            dma((3,)), dma((3,)), dma((25,)), dma((25,)),
        ],
        compiler_params=pltpu.CompilerParams(
            collective_id=0, has_side_effects=True, vmem_limit_bytes=40 * 1024 * 1024
        ),
    )(*[pltpu.with_memory_space_constraint(array, pltpu.HBM) for array in arrays])
    grad_input, down, gain, shift = pl.pallas_call(
        write,
        out_shape=(
            jax.ShapeDtypeStruct((2, 32, 128, 128), BF),
            jax.ShapeDtypeStruct((27, 1, 128), F32),
            jax.ShapeDtypeStruct((4,), F32),
            jax.ShapeDtypeStruct((4,), F32),
        ),
        in_specs=[vmem] * 3,
        out_specs=(hbm, hbm, smem, smem),
        scratch_shapes=[dma((2,))],
        compiler_params=pltpu.CompilerParams(vmem_limit_bytes=2 * 1024 * 1024),
    )(grad_input, down, stat)
    return (grad_input, down.transpose(1, 0, 2), gain, shift)


def solution(mesh):
    return jax.shard_map(
        local,
        mesh=mesh,
        in_specs=(
            P("slab", "grp", None, None),
            P("slab", "grp", None, None),
            P("slab", None, "grp"),
            P("slab", None, "grp"),
            P("slab"),
            P(),
            P(),
        ),
        out_specs=(
            P("slab", "grp", None, None),
            P(("slab", "grp"), None, None),
            P("slab"),
            P("slab"),
        ),
        check_vma=False,
    )
```

```python
import functools
import math

import jax
import jax.numpy as jnp
from jax import lax
from jax.experimental import pallas as pl
from jax.experimental.pallas import tpu as pltpu
from jax.sharding import PartitionSpec as P

MESH = pl.DeviceIdType.MESH
BF, F32 = jnp.bfloat16, jnp.float32
NT = (((1,), (1,)), ((), ()))
REACH = (((1, 0),), ((2, 0), (0, 1)))


def device(x, y, z, core):
    return (x * 16 + z * 2 + y // 2, y % 2 * 2 + core)


def remote(src, dst, send, recv, where):
    return pltpu.make_async_remote_copy(
        src_ref=src, dst_ref=dst, send_sem=send, recv_sem=recv, device_id=where, device_id_type=MESH
    )


def kernel(
    cells, scale,
    fine_hbm, og_hbm, pn_hbm, act_hbm, gain_hbm, wd_hbm, wu_hbm,
    gin, down_ref, stat_ref,
    fine, og, pn, act, wd, wu, gain_ref, rows32, taps_up, deep32, grad8,
    a1_out, a1_in, a2_out, a2_in, h_in, pn32, act32, moment, term,
    fine_edge, f_even, f_odd, g_own, g_next, gt, gts, q, o32,
    pair_out, pair_in, ax, ax_in, by, by_in, ay, ay_in, ay_own, zz, zs, zs_in,
    load, a1_send, a1_recv, a2_send, a2_recv, h_send, h_recv, m_send, m_recv, t_send, t_recv,
    edge_send, edge_recv, rs_send, rs_recv,
):
    slab, grp = lax.axis_index("slab"), lax.axis_index("grp")
    x, y, z, core = slab // 16, slab % 2 * 2 + grp // 2, slab // 2 % 8, grp % 2
    loads = [
        pltpu.make_async_copy(src, dst, load.at[i])
        for i, (src, dst) in enumerate(
            ((og_hbm, og), (wu_hbm, wu), (fine_hbm, fine), (pn_hbm, pn), (act_hbm, act), (wd_hbm, wd), (gain_hbm, gain_ref))
        )
    ]
    for copy in loads:
        copy.start()
    barrier = pltpu.get_barrier_semaphore()

    def greet(d, carry):
        pl.semaphore_signal(barrier, inc=1, device_id=((slab + d) % 64, grp), device_id_type=MESH)
        return carry

    lax.fori_loop(1, 64, greet, 0)
    for d in (1, 2, 3):
        pl.semaphore_signal(barrier, inc=1, device_id=(slab, (grp + d) % 4), device_id_type=MESH)
    for d in range(1, 8):
        cross = ((x + d // 2) % 4 * 16 + z * 2 + (slab + d) % 2, (grp + 2) % 4)
        pl.semaphore_signal(barrier, inc=1, device_id=cross, device_id_type=MESH)

    low = lax.broadcasted_iota(jnp.int32, (8, 512), 0) < 4

    loads[0].wait()
    loads[1].wait()
    for side in range(4):
        taps_up[side] = jnp.concatenate([wu[2 * side], wu[2 * side + 1]], axis=1)

    def part(row, carry):
        for side in range(4):
            rows32[side] = og[side // 2, 2 * row + side % 2].astype(F32)
            at = pl.ds(pl.multiple_of(row * 64, 64), 64)
            grad8[side, at, 0:128] = rows32[side, pl.ds(0, 64, stride=2), :].astype(BF)
            grad8[side, at, 128:256] = rows32[side, pl.ds(1, 64, stride=2), :].astype(BF)
        return carry

    lax.fori_loop(0, 16, part, 0)
    total = lax.dot_general(taps_up[0], grad8[0], NT, preferred_element_type=F32)
    for side in range(1, 4):
        total = total + lax.dot_general(taps_up[side], grad8[side], NT, preferred_element_type=F32)
    deep32[...] = total

    def pieces_of(m, carry):
        at = pl.ds(pl.multiple_of(m * 8, 8), 8)
        left, right = deep32[at, 0:512], deep32[at, 512:1024]
        a1_out[2 * m] = jnp.where(low, left, pltpu.roll(right, 4, 0)).astype(BF)
        a1_out[2 * m + 1] = jnp.where(low, pltpu.roll(left, 4, 0), right).astype(BF)
        return carry

    lax.fori_loop(0, 32, pieces_of, 0)
    pl.semaphore_wait(barrier, 73)

    def target(d):
        return (slab + d) % 64

    def origin(d):
        return (slab + 64 - d) % 64

    def a1_copy(d):
        to = target(d)
        return remote(a1_out.at[to], a1_in.at[slab], a1_send.at[d], a1_recv.at[d], (to, grp))

    def a1_start(d, carry):
        a1_copy(d).start()
        return carry

    lax.fori_loop(1, 64, a1_start, 0)
    a1_in[slab] = a1_out[slab]

    loads[2].wait()
    edge = remote(fine.at[:, 31], fine_edge, edge_send.at[0], edge_recv.at[0], (slab, (grp + 1) % 4))
    edge.start()
    loads[3].wait()
    loads[4].wait()
    loads[6].wait()
    for ch in range(4):
        for half in range(2):
            for block in range(4):
                lanes = slice(half * 512 + block * 128, half * 512 + block * 128 + 128)
                pn32[block, pl.ds(half * 4 + ch, 64, stride=8), :] = pn[ch, :, lanes].astype(F32)
                act32[block, pl.ds(half * 4 + ch, 64, stride=8), :] = act[ch, :, lanes].astype(F32)

    def wide(ref, i):
        at = pl.ds(pl.multiple_of(i * 8, 8), 8)
        return jnp.concatenate([ref[block, at, :] for block in range(4)], axis=1)

    def spread(rows):
        per_row = jnp.sum(rows, axis=1, keepdims=True)
        per_row = jnp.broadcast_to(per_row, (8, 128))
        return per_row + pltpu.roll(per_row, 4, 0)

    def moments(i, carry):
        value = wide(pn32, i)
        return carry[0] + value, carry[1] + value * value

    none = jnp.zeros((8, 512), F32)
    one, two = lax.fori_loop(0, 64, moments, (none, none))
    moment[grp, 0] = spread(one)
    moment[grp, 1] = spread(two)
    m_copies = []
    for d in (1, 2, 3):
        m_copies.append(remote(moment.at[grp], moment.at[grp], m_send.at[d], m_recv.at[d], (slab, (grp + d) % 4)))
        m_copies[-1].start()

    first_row = lax.broadcasted_iota(jnp.int32, (64, 128), 0) == 0

    def place_row(slot, block, values, at):
        rows32[slot] = values.astype(F32)
        even = rows32[slot, pl.ds(0, 64, stride=2), :]
        odd = rows32[slot, pl.ds(1, 64, stride=2), :]
        block[at, 0:128] = jnp.where(first_row, 0.0, pltpu.roll(odd, 1, 0)).astype(BF)
        block[at, 128:256] = even.astype(BF)
        block[at, 256:384] = odd.astype(BF)

    def split_fine(row, carry):
        for plane in range(2):
            place_row(2 * plane, f_even.at[plane], fine[plane, 2 * row], pl.ds(pl.multiple_of(row * 64, 64), 64))
            place_row(
                2 * plane + 1, f_odd.at[plane], fine[plane, 2 * row + 1],
                pl.ds(pl.multiple_of(row * 64 + 64, 64), 64),
            )
        return carry

    lax.fori_loop(0, 16, split_fine, 0)
    edge.wait()
    for plane in range(2):
        behind = fine_edge[plane].astype(F32)
        place_row(plane, f_odd.at[plane], jnp.where(grp == 0, jnp.zeros_like(behind), behind), pl.ds(0, 64))
    for copy in m_copies:
        copy.wait()
    sums = moment[0] + moment[1] + moment[2] + moment[3]
    mean = sums[0] / cells
    inv_std = lax.rsqrt(sums[1] / cells - mean * mean + 1e-05)
    mean_w, inv_w = jnp.tile(mean, (1, 4)), jnp.tile(inv_std, (1, 4))

    def masked_of(i):
        normed = (wide(pn32, i) - mean_w) * inv_w
        masked = jnp.where(wide(act32, i) > 0, a1_in[i].astype(F32), 0.0)
        return masked, normed

    def terms(i, carry):
        masked, normed = masked_of(i)
        return carry[0] + masked, carry[1] + masked * normed

    def a1_wait(d, carry):
        a1_copy(d).wait()
        return terms(origin(d), carry)

    one, two = lax.fori_loop(1, 64, a1_wait, terms(slab, (none, none)))
    term[grp, 0] = spread(one)
    term[grp, 1] = spread(two)
    t_copies = []
    for d in (1, 2, 3):
        t_copies.append(remote(term.at[grp], term.at[grp], t_send.at[d], t_recv.at[d], (slab, (grp + d) % 4)))
        t_copies[-1].start()
    for copy in t_copies:
        copy.wait()
    sums = term[0] + term[1] + term[2] + term[3]
    shift, gain = sums[0] / cells, sums[1] / cells
    stat_ref[0] = gain
    stat_ref[1] = shift
    shift_w, gain_w = jnp.tile(shift, (1, 4)), jnp.tile(gain, (1, 4))
    channel = lax.broadcasted_iota(jnp.int32, (8, 128), 0) % 4
    norm_gain = jnp.full((8, 128), gain_ref[0], F32)
    for ch in range(1, 4):
        norm_gain = jnp.where(channel == ch, gain_ref[ch], norm_gain)
    factor_w = jnp.tile(norm_gain * inv_std, (1, 4))

    def act_grad(i):
        masked, normed = masked_of(i)
        a2_out[i] = (factor_w * (masked - shift_w - normed * gain_w)).astype(BF)

    def a2_copy(d):
        to = target(d)
        return remote(a2_out.at[to], a2_in.at[slab], a2_send.at[d], a2_recv.at[d], (to, grp))

    def a2_start(d, carry):
        act_grad(target(d))
        a2_copy(d - 1).start()
        return carry

    act_grad(target(1))
    lax.fori_loop(2, 64, a2_start, 0)
    act_grad(slab)
    a2_copy(63).start()
    a2_in[slab] = a2_out[slab]

    def on_copy(d):
        source = origin(d)
        return remote(
            a2_in.at[source], h_in.at[source], h_send.at[d], h_recv.at[d], ((slab + 63) % 64, grp)
        )

    def a2_wait(d, carry):
        a2_copy(d).wait()
        on_copy(d).start()
        return carry

    on_copy(0).start()
    loads[5].wait()
    lax.fori_loop(1, 64, a2_wait, 0)

    def join(source, block, keep=None):
        def pair_of(m):
            a, b = source[2 * m].astype(F32), source[2 * m + 1].astype(F32)
            left = jnp.where(low, a, pltpu.roll(b, 4, 0))
            right = jnp.where(low, pltpu.roll(a, 4, 0), b)
            return jnp.concatenate([left, right], axis=1)

        def step(m, carry):
            at = pl.ds(pl.multiple_of(m * 16, 16), 16)
            found = jnp.concatenate([pair_of(2 * m), pair_of(2 * m + 1)], axis=0)
            if keep is not None:
                found = jnp.where(keep, found, jnp.zeros_like(found))
            block[at, :] = found.astype(BF)
            return carry

        lax.fori_loop(0, 16, step, 0)

    def tap_grads(kx, block, plane, rows=(0, 1, 2)):
        for ky in rows:
            window = f_even[plane] if ky == 1 else f_odd[plane, ky * 32 : ky * 32 + 1024]
            found = jnp.dot(block[...], window, preferred_element_type=F32)
            for kz in range(3):
                q[9 * kx + 3 * ky + kz] = found[:, kz * 128 : kz * 128 + 128]

    last_cell = lax.broadcasted_iota(jnp.int32, (128, 256), 0) % 64 == 63
    last_row = lax.broadcasted_iota(jnp.int32, (64, 256), 0) == 63

    def turn(block, plane):
        for part in range(8):
            turned = jnp.transpose(block[:, part * 128 : part * 128 + 128].astype(F32))
            gt[plane, part * 128 : part * 128 + 128] = turned.astype(BF)
            moved = jnp.where(last_cell, 0.0, pltpu.roll(turned, 127, 0))
            gts[plane, part * 128 : part * 128 + 128] = moved.astype(BF)

    def edge_row(plane):
        return remote(
            gt.at[plane, 0:64], gt.at[plane, 1024:1088], edge_send.at[1 + plane], edge_recv.at[1 + plane],
            (slab, (grp + 3) % 4),
        )

    def finish_edge(plane):
        edge_row(plane).wait()
        after = gt[plane, 1024:1088].astype(F32)
        after = jnp.where(grp == 3, jnp.zeros_like(after), after)
        gt[plane, 1024:1088] = after.astype(BF)
        gts[plane, 1024:1088] = jnp.where(last_row, 0.0, pltpu.roll(after, 63, 0)).astype(BF)

    def input_grad(px, py, begin=0, end=4):
        def chunk(c, carry):
            both = jnp.zeros((256, 256), F32)
            odd = jnp.zeros((256, 128), F32)
            for kx, off_x in REACH[px]:
                for ky, off_y in REACH[py]:
                    at = pl.ds(pl.multiple_of(c * 256 + off_y * 64, 64), 256)
                    tap = 9 * kx + 3 * ky
                    pair = wd[tap + 1 : tap + 3].reshape(256, 256)
                    both = both + lax.dot_general(gt[off_x, at], pair, NT, preferred_element_type=F32)
                    odd = odd + lax.dot_general(gts[off_x, at], wd[tap], NT, preferred_element_type=F32)
            o32[pl.ds(0, 256, stride=2), :] = both[:, 0:128]
            o32[pl.ds(1, 256, stride=2), :] = both[:, 128:256] + odd
            for row in range(4):
                gin[px, 8 * c + 2 * row + py] = o32[row * 128 : row * 128 + 128].astype(BF)
            return carry

        lax.fori_loop(begin, end, chunk, 0)

    def pack(first, slot, count=9):
        def step(i, carry):
            for side in range(4):
                found = q[first + i, pl.ds(side * 2 + 1 - core, 32, stride=8), :]
                pair_out[slot + i, side] = found.astype(BF).reshape(4, 8, 128)
            return carry

        lax.fori_loop(0, count, step, 0)

    def pair_copy(part, slot, count):
        at = pl.ds(slot, count)
        return remote(
            pair_out.at[at], pair_in.at[at], rs_send.at[part], rs_recv.at[part], (slab, grp + 1 - 2 * core)
        )

    def held(tap, slot, side):
        found = q[tap, pl.ds(side * 2 + core, 32, stride=8), :].reshape(4, 8, 128)
        return found + pair_in[slot, side].astype(F32)

    def ax_copy(part, d):
        to, i, at = (x + d) % 4, 4 + part * 3 + d, pl.ds(part * 9, 9)
        return remote(ax.at[to, at], ax_in.at[d - 1, at], rs_send.at[i], rs_recv.at[i], device(to, y, z, core))

    def ay_copy(part, d):
        to, i, at = (y + d) % 4, 10 + part * 18 + d, pl.ds(part * 9, 9)
        return remote(ay.at[to, at], ay_in.at[d - 1, at], rs_send.at[i], rs_recv.at[i], device(x, to, z, core))

    def by_copy(d):
        to_x, to_y, i = (x + d // 4) % 4, (y + d % 4) % 4, 13 + d
        return remote(
            by.at[to_x * 4 + to_y], by_in.at[d - 1], rs_send.at[i], rs_recv.at[i], device(to_x, to_y, z, core)
        )

    def add_x(slot, carry):
        found = ax[x, slot].astype(F32)
        for d in range(3):
            found = found + ax_in[d, slot].astype(F32)
        ay_own[slot] = found
        for block in range(4):
            ay[block, slot] = found[block].astype(BF)
        return carry

    def split_x(part):
        def step(i, carry):
            slot = part * 9 + i
            for side in range(4):
                found = held(9 + slot, slot, side).astype(BF)
                for block in range(4):
                    ax[block, slot, side] = found[block]
            return carry

        lax.fori_loop(0, 9, step, 0)

    join(a2_in, g_own)
    tap_grads(1, g_own, 0)
    pack(9, 0)
    pair_copy(0, 0, 9).start()
    tap_grads(2, g_own, 1)
    pack(18, 9)
    pair_copy(1, 9, 9).start()

    def first_wave(part):
        pair_copy(part, part * 9, 9).wait()
        split_x(part)
        for d in (1, 2, 3):
            ax_copy(part, d).start()

    def second_wave(part):
        for d in (1, 2, 3):
            ax_copy(part, d).wait()
        lax.fori_loop(part * 9, part * 9 + 9, add_x, 0)
        for d in (1, 2, 3):
            ay_copy(part, d).start()

    first_wave(0)
    turn(g_own, 0)
    edge_row(0).start()
    first_wave(1)
    finish_edge(0)
    input_grad(0, 0)
    second_wave(0)
    input_grad(0, 1)

    def on_wait(d, carry):
        on_copy(d).wait()
        return carry

    lax.fori_loop(0, 64, on_wait, 0)
    join(h_in, g_next, slab != 63)
    for ky in range(3):
        tap_grads(0, g_next, 1, (ky,))
        pack(3 * ky, 18 + 3 * ky, 3)
        pair_copy(2 + ky, 18 + 3 * ky, 3).start()
    turn(g_next, 1)
    edge_row(1).start()

    def split_y(i, carry):
        for side in range(4):
            found = held(i, 18 + i, side).astype(BF)
            for block in range(4):
                by[block * 4 + side, i] = found[block]
        return carry

    for ky in range(3):
        pair_copy(2 + ky, 18 + 3 * ky, 3).wait()
        lax.fori_loop(3 * ky, 3 * ky + 3, split_y, 0)
    for d in range(1, 16):
        by_copy(d).start()
    second_wave(1)
    finish_edge(1)
    input_grad(1, 0)
    input_grad(1, 1, 0, 2)
    for part in range(2):
        for d in (1, 2, 3):
            ay_copy(part, d).wait()
    for d in range(1, 16):
        by_copy(d).wait()
    own = x * 4 + y
    for tap in range(27):
        if tap < 9:
            found = by[own, tap].astype(F32)
            for d in range(15):
                found = found + by_in[d, tap].astype(F32)
        else:
            t = tap - 9
            found = ay_own[t, y]
            for d in range(3):
                found = found + ay_in[d, t].astype(F32)
        zz[tap * 8 : tap * 8 + 8, :] = found
    for row in range(8):
        zs[row] = zz[pl.ds(row, 27, stride=8), :].astype(BF)
    def z_copy(d):
        to, i = (z + d) % 8, 31 + d
        return remote(zs.at[to], zs_in.at[d - 1], rs_send.at[i], rs_recv.at[i], device(x, y, to, core))

    for d in range(1, 8):
        z_copy(d).start()
    input_grad(1, 1, 2, 4)
    for d in range(1, 8):
        z_copy(d).wait()
    found = zz[pl.ds(z, 27, stride=8), :]
    for d in range(7):
        found = found + zs_in[d].astype(F32)
    for tap in range(27):
        down_ref[tap] = found[tap : tap + 1] * scale


def write(gin, down, stat, gin_out, down_out, gain_out, shift_out, sem):
    copies = [
        pltpu.make_async_copy(gin, gin_out, sem.at[0]),
        pltpu.make_async_copy(down, down_out, sem.at[1]),
    ]
    for copy in copies:
        copy.start()
    row = lax.broadcasted_iota(jnp.int32, (8, 128), 0)
    lane = lax.broadcasted_iota(jnp.int32, (8, 128), 1)
    for ch in range(4):
        here = (row == ch) & (lane == 0)
        gain_out[ch] = jnp.sum(jnp.where(here, stat[0], 0.0))
        shift_out[ch] = jnp.sum(jnp.where(here, stat[1], 0.0))
    for copy in copies:
        copy.wait()


def local(fine_input, out_grad, pre_norm, act_out, norm_gain, w_down, w_up):
    cells = pre_norm.shape[1] * pre_norm.shape[2] * lax.axis_size("grp")
    arrays = (fine_input, out_grad, pre_norm, act_out, norm_gain, w_down, w_up)
    vmem = pl.BlockSpec(memory_space=pltpu.VMEM)
    smem = pl.BlockSpec(memory_space=pltpu.SMEM)
    hbm = pl.BlockSpec(memory_space=pltpu.HBM)
    dma = pltpu.SemaphoreType.DMA
    grad_input, down, stat = pl.pallas_call(
        functools.partial(kernel, float(cells), 1.0 / math.sqrt(cells)),
        out_shape=(
            jax.ShapeDtypeStruct((2, 32, 128, 128), BF),
            jax.ShapeDtypeStruct((27, 1, 128), F32),
            jax.ShapeDtypeStruct((2, 8, 128), F32),
        ),
        in_specs=[hbm] * 7,
        out_specs=(vmem, vmem, vmem),
        scratch_shapes=[
            pltpu.VMEM((2, 32, 128, 128), BF),
            pltpu.VMEM((2, 32, 128, 128), BF),
            pltpu.VMEM((4, 64, 1024), BF),
            pltpu.VMEM((4, 64, 1024), BF),
            pltpu.VMEM((27, 128, 256), BF),
            pltpu.VMEM((8, 256, 128), BF),
            pltpu.SMEM((4,), F32),
            pltpu.VMEM((4, 128, 128), F32),
            pltpu.VMEM((4, 256, 256), BF),
            pltpu.VMEM((256, 1024), F32),
            pltpu.VMEM((4, 1024, 256), BF),
            pltpu.VMEM((64, 8, 512), BF),
            pltpu.VMEM((64, 8, 512), BF),
            pltpu.VMEM((64, 8, 512), BF),
            pltpu.VMEM((64, 8, 512), BF),
            pltpu.VMEM((64, 8, 512), BF),
            pltpu.VMEM((4, 512, 128), F32),
            pltpu.VMEM((4, 512, 128), F32),
            pltpu.VMEM((4, 2, 8, 128), F32),
            pltpu.VMEM((4, 2, 8, 128), F32),
            pltpu.VMEM((2, 128, 128), BF),
            pltpu.VMEM((2, 1024, 384), BF),
            pltpu.VMEM((2, 1088, 384), BF),
            pltpu.VMEM((256, 1024), BF),
            pltpu.VMEM((256, 1024), BF),
            pltpu.VMEM((2, 1088, 256), BF),
            pltpu.VMEM((2, 1088, 256), BF),
            pltpu.VMEM((27, 256, 128), F32),
            pltpu.VMEM((512, 128), F32),
            pltpu.VMEM((27, 4, 4, 8, 128), BF),
            pltpu.VMEM((27, 4, 4, 8, 128), BF),
            pltpu.VMEM((4, 18, 4, 8, 128), BF),
            pltpu.VMEM((3, 18, 4, 8, 128), BF),
            pltpu.VMEM((16, 9, 8, 128), BF),
            pltpu.VMEM((15, 9, 8, 128), BF),
            pltpu.VMEM((4, 18, 8, 128), BF),
            pltpu.VMEM((3, 18, 8, 128), BF),
            pltpu.VMEM((18, 4, 8, 128), F32),
            pltpu.VMEM((216, 128), F32),
            pltpu.VMEM((8, 27, 128), BF),
            pltpu.VMEM((7, 27, 128), BF),
            dma((7,)),
            dma((64,)), dma((64,)), dma((64,)), dma((64,)), dma((64,)), dma((64,)),
            dma((4,)), dma((4,)), dma((4,)), dma((4,)),
            dma((3,)), dma((3,)), dma((40,)), dma((40,)),
        ],
        compiler_params=pltpu.CompilerParams(
            collective_id=0, has_side_effects=True, vmem_limit_bytes=40 * 1024 * 1024
        ),
    )(*[pltpu.with_memory_space_constraint(array, pltpu.HBM) for array in arrays])
    grad_input, down, gain, shift = pl.pallas_call(
        write,
        out_shape=(
            jax.ShapeDtypeStruct((2, 32, 128, 128), BF),
            jax.ShapeDtypeStruct((27, 1, 128), F32),
            jax.ShapeDtypeStruct((4,), F32),
            jax.ShapeDtypeStruct((4,), F32),
        ),
        in_specs=[vmem] * 3,
        out_specs=(hbm, hbm, smem, smem),
        scratch_shapes=[dma((2,))],
        compiler_params=pltpu.CompilerParams(vmem_limit_bytes=2 * 1024 * 1024),
    )(grad_input, down, stat)
    return (grad_input, down.transpose(1, 0, 2), gain, shift)


def solution(mesh):
    return jax.shard_map(
        local,
        mesh=mesh,
        in_specs=(
            P("slab", "grp", None, None),
            P("slab", "grp", None, None),
            P("slab", None, "grp"),
            P("slab", None, "grp"),
            P("slab"),
            P(),
            P(),
        ),
        out_specs=(
            P("slab", "grp", None, None),
            P(("slab", "grp"), None, None),
            P("slab"),
            P("slab"),
        ),
        check_vma=False,
    )
```

```python
import functools
import math

import jax
import jax.numpy as jnp
from jax import lax
from jax.experimental import pallas as pl
from jax.experimental.pallas import tpu as pltpu
from jax.sharding import PartitionSpec as P

MESH = pl.DeviceIdType.MESH
BF, F32 = jnp.bfloat16, jnp.float32
NT = (((1,), (1,)), ((), ()))
REACH = (((1, 0),), ((2, 0), (0, 1)))


def device(x, y, z, core):
    return (x * 16 + z * 2 + y // 2, y % 2 * 2 + core)


def remote(src, dst, send, recv, where):
    return pltpu.make_async_remote_copy(
        src_ref=src, dst_ref=dst, send_sem=send, recv_sem=recv, device_id=where, device_id_type=MESH
    )


def kernel(
    cells, scale,
    fine_hbm, og_hbm, pn_hbm, act_hbm, gain_hbm, wd_hbm, wu_hbm,
    gin, down_ref, stat_ref,
    fine, og, pn, act, wd, wu, gain_ref, rows32, taps_up, deep32, grad8,
    a1_out, a1_in, a2_out, a2_in, h_in, pn32, act32, moment, term,
    fine_edge, f_even, f_odd, g_own, g_next, gt, gts, q, o32,
    pair_out, pair_in, ax, ax_in, by, by_in, ay, ay_in, ay_own, zz, zs, zs_in,
    load, a1_send, a1_recv, a2_send, a2_recv, h_send, h_recv, m_send, m_recv, t_send, t_recv,
    edge_send, edge_recv, rs_send, rs_recv,
):
    slab, grp = lax.axis_index("slab"), lax.axis_index("grp")
    x, y, z, core = slab // 16, slab % 2 * 2 + grp // 2, slab // 2 % 8, grp % 2
    loads = [
        pltpu.make_async_copy(src, dst, load.at[i])
        for i, (src, dst) in enumerate(
            ((og_hbm, og), (wu_hbm, wu), (fine_hbm, fine), (pn_hbm, pn), (act_hbm, act), (wd_hbm, wd), (gain_hbm, gain_ref))
        )
    ]
    for copy in loads:
        copy.start()
    barrier = pltpu.get_barrier_semaphore()

    def greet(d, carry):
        pl.semaphore_signal(barrier, inc=1, device_id=((slab + d) % 64, grp), device_id_type=MESH)
        return carry

    lax.fori_loop(1, 64, greet, 0)
    for d in (1, 2, 3):
        pl.semaphore_signal(barrier, inc=1, device_id=(slab, (grp + d) % 4), device_id_type=MESH)
    for d in range(1, 8):
        cross = ((x + d // 2) % 4 * 16 + z * 2 + (slab + d) % 2, (grp + 2) % 4)
        pl.semaphore_signal(barrier, inc=1, device_id=cross, device_id_type=MESH)

    low = lax.broadcasted_iota(jnp.int32, (8, 512), 0) < 4

    loads[0].wait()
    loads[1].wait()
    for side in range(4):
        taps_up[side] = jnp.concatenate([wu[2 * side], wu[2 * side + 1]], axis=1)

    def part(row, carry):
        for side in range(4):
            rows32[side] = og[side // 2, 2 * row + side % 2].astype(F32)
            at = pl.ds(pl.multiple_of(row * 64, 64), 64)
            grad8[side, at, 0:128] = rows32[side, pl.ds(0, 64, stride=2), :].astype(BF)
            grad8[side, at, 128:256] = rows32[side, pl.ds(1, 64, stride=2), :].astype(BF)
        return carry

    lax.fori_loop(0, 16, part, 0)
    total = lax.dot_general(taps_up[0], grad8[0], NT, preferred_element_type=F32)
    for side in range(1, 4):
        total = total + lax.dot_general(taps_up[side], grad8[side], NT, preferred_element_type=F32)
    deep32[...] = total

    def pieces_of(m, carry):
        at = pl.ds(pl.multiple_of(m * 8, 8), 8)
        left, right = deep32[at, 0:512], deep32[at, 512:1024]
        a1_out[2 * m] = jnp.where(low, left, pltpu.roll(right, 4, 0)).astype(BF)
        a1_out[2 * m + 1] = jnp.where(low, pltpu.roll(left, 4, 0), right).astype(BF)
        return carry

    lax.fori_loop(0, 32, pieces_of, 0)
    pl.semaphore_wait(barrier, 73)

    def target(d):
        return (slab + d) % 64

    def origin(d):
        return (slab + 64 - d) % 64

    def a1_copy(d):
        to = target(d)
        return remote(a1_out.at[to], a1_in.at[slab], a1_send.at[d], a1_recv.at[d], (to, grp))

    def a1_start(d, carry):
        a1_copy(d).start()
        return carry

    lax.fori_loop(1, 64, a1_start, 0)
    a1_in[slab] = a1_out[slab]

    loads[2].wait()
    edge = remote(fine.at[:, 31], fine_edge, edge_send.at[0], edge_recv.at[0], (slab, (grp + 1) % 4))
    edge.start()
    loads[3].wait()
    loads[4].wait()
    loads[6].wait()
    for ch in range(4):
        for half in range(2):
            for block in range(4):
                lanes = slice(half * 512 + block * 128, half * 512 + block * 128 + 128)
                pn32[block, pl.ds(half * 4 + ch, 64, stride=8), :] = pn[ch, :, lanes].astype(F32)
                act32[block, pl.ds(half * 4 + ch, 64, stride=8), :] = act[ch, :, lanes].astype(F32)

    def wide(ref, i):
        at = pl.ds(pl.multiple_of(i * 8, 8), 8)
        return jnp.concatenate([ref[block, at, :] for block in range(4)], axis=1)

    def spread(rows):
        per_row = jnp.sum(rows, axis=1, keepdims=True)
        per_row = jnp.broadcast_to(per_row, (8, 128))
        return per_row + pltpu.roll(per_row, 4, 0)

    def moments(i, carry):
        value = wide(pn32, i)
        return carry[0] + value, carry[1] + value * value

    none = jnp.zeros((8, 512), F32)
    one, two = lax.fori_loop(0, 64, moments, (none, none))
    moment[grp, 0] = spread(one)
    moment[grp, 1] = spread(two)
    m_copies = []
    for d in (1, 2, 3):
        m_copies.append(remote(moment.at[grp], moment.at[grp], m_send.at[d], m_recv.at[d], (slab, (grp + d) % 4)))
        m_copies[-1].start()

    first_row = lax.broadcasted_iota(jnp.int32, (64, 128), 0) == 0

    def place_row(slot, block, values, at):
        rows32[slot] = values.astype(F32)
        even = rows32[slot, pl.ds(0, 64, stride=2), :]
        odd = rows32[slot, pl.ds(1, 64, stride=2), :]
        block[at, 0:128] = jnp.where(first_row, 0.0, pltpu.roll(odd, 1, 0)).astype(BF)
        block[at, 128:256] = even.astype(BF)
        block[at, 256:384] = odd.astype(BF)

    def split_fine(row, carry):
        for plane in range(2):
            place_row(2 * plane, f_even.at[plane], fine[plane, 2 * row], pl.ds(pl.multiple_of(row * 64, 64), 64))
            place_row(
                2 * plane + 1, f_odd.at[plane], fine[plane, 2 * row + 1],
                pl.ds(pl.multiple_of(row * 64 + 64, 64), 64),
            )
        return carry

    lax.fori_loop(0, 16, split_fine, 0)
    edge.wait()
    for plane in range(2):
        behind = fine_edge[plane].astype(F32)
        place_row(plane, f_odd.at[plane], jnp.where(grp == 0, jnp.zeros_like(behind), behind), pl.ds(0, 64))
    for copy in m_copies:
        copy.wait()
    sums = moment[0] + moment[1] + moment[2] + moment[3]
    mean = sums[0] / cells
    inv_std = lax.rsqrt(sums[1] / cells - mean * mean + 1e-05)
    mean_w, inv_w = jnp.tile(mean, (1, 4)), jnp.tile(inv_std, (1, 4))

    def masked_of(i):
        normed = (wide(pn32, i) - mean_w) * inv_w
        masked = jnp.where(wide(act32, i) > 0, a1_in[i].astype(F32), 0.0)
        return masked, normed

    def terms(i, carry):
        masked, normed = masked_of(i)
        return carry[0] + masked, carry[1] + masked * normed

    def a1_wait(d, carry):
        a1_copy(d).wait()
        return terms(origin(d), carry)

    one, two = lax.fori_loop(1, 64, a1_wait, terms(slab, (none, none)))
    term[grp, 0] = spread(one)
    term[grp, 1] = spread(two)
    t_copies = []
    for d in (1, 2, 3):
        t_copies.append(remote(term.at[grp], term.at[grp], t_send.at[d], t_recv.at[d], (slab, (grp + d) % 4)))
        t_copies[-1].start()
    for copy in t_copies:
        copy.wait()
    sums = term[0] + term[1] + term[2] + term[3]
    shift, gain = sums[0] / cells, sums[1] / cells
    stat_ref[0] = gain
    stat_ref[1] = shift
    shift_w, gain_w = jnp.tile(shift, (1, 4)), jnp.tile(gain, (1, 4))
    channel = lax.broadcasted_iota(jnp.int32, (8, 128), 0) % 4
    norm_gain = jnp.full((8, 128), gain_ref[0], F32)
    for ch in range(1, 4):
        norm_gain = jnp.where(channel == ch, gain_ref[ch], norm_gain)
    factor_w = jnp.tile(norm_gain * inv_std, (1, 4))

    def act_grad(i):
        masked, normed = masked_of(i)
        a2_out[i] = (factor_w * (masked - shift_w - normed * gain_w)).astype(BF)

    def a2_copy(d):
        to = target(d)
        return remote(a2_out.at[to], a2_in.at[slab], a2_send.at[d], a2_recv.at[d], (to, grp))

    def a2_start(d, carry):
        act_grad(target(d))
        a2_copy(d - 1).start()
        return carry

    act_grad(target(1))
    lax.fori_loop(2, 64, a2_start, 0)
    act_grad(slab)
    a2_copy(63).start()
    a2_in[slab] = a2_out[slab]

    def on_copy(d):
        source = origin(d)
        return remote(
            a2_in.at[source], h_in.at[source], h_send.at[d], h_recv.at[d], ((slab + 63) % 64, grp)
        )

    def a2_wait(d, carry):
        a2_copy(d).wait()
        on_copy(d).start()
        return carry

    on_copy(0).start()
    loads[5].wait()
    lax.fori_loop(1, 64, a2_wait, 0)

    def join(source, block, keep=None):
        def pair_of(m):
            a, b = source[2 * m].astype(F32), source[2 * m + 1].astype(F32)
            left = jnp.where(low, a, pltpu.roll(b, 4, 0))
            right = jnp.where(low, pltpu.roll(a, 4, 0), b)
            return jnp.concatenate([left, right], axis=1)

        def step(m, carry):
            at = pl.ds(pl.multiple_of(m * 16, 16), 16)
            found = jnp.concatenate([pair_of(2 * m), pair_of(2 * m + 1)], axis=0)
            if keep is not None:
                found = jnp.where(keep, found, jnp.zeros_like(found))
            block[at, :] = found.astype(BF)
            return carry

        lax.fori_loop(0, 16, step, 0)

    def tap_grads(kx, block, plane, rows=(0, 1, 2)):
        for ky in rows:
            window = f_even[plane] if ky == 1 else f_odd[plane, ky * 32 : ky * 32 + 1024]
            found = jnp.dot(block[...], window, preferred_element_type=F32)
            for kz in range(3):
                q[9 * kx + 3 * ky + kz] = found[:, kz * 128 : kz * 128 + 128]

    last_cell = lax.broadcasted_iota(jnp.int32, (128, 256), 0) % 64 == 63
    last_row = lax.broadcasted_iota(jnp.int32, (64, 256), 0) == 63

    def turn(block, plane):
        for part in range(8):
            turned = jnp.transpose(block[:, part * 128 : part * 128 + 128].astype(F32))
            gt[plane, part * 128 : part * 128 + 128] = turned.astype(BF)
            moved = jnp.where(last_cell, 0.0, pltpu.roll(turned, 127, 0))
            gts[plane, part * 128 : part * 128 + 128] = moved.astype(BF)

    def edge_row(plane):
        return remote(
            gt.at[plane, 0:64], gt.at[plane, 1024:1088], edge_send.at[1 + plane], edge_recv.at[1 + plane],
            (slab, (grp + 3) % 4),
        )

    def finish_edge(plane):
        edge_row(plane).wait()
        after = gt[plane, 1024:1088].astype(F32)
        after = jnp.where(grp == 3, jnp.zeros_like(after), after)
        gt[plane, 1024:1088] = after.astype(BF)
        gts[plane, 1024:1088] = jnp.where(last_row, 0.0, pltpu.roll(after, 63, 0)).astype(BF)

    def input_grad(px, py, begin=0, end=4):
        def chunk(c, carry):
            both = jnp.zeros((256, 256), F32)
            odd = jnp.zeros((256, 128), F32)
            for kx, off_x in REACH[px]:
                for ky, off_y in REACH[py]:
                    at = pl.ds(pl.multiple_of(c * 256 + off_y * 64, 64), 256)
                    tap = 9 * kx + 3 * ky
                    pair = wd[tap + 1 : tap + 3].reshape(256, 256)
                    both = both + lax.dot_general(gt[off_x, at], pair, NT, preferred_element_type=F32)
                    odd = odd + lax.dot_general(gts[off_x, at], wd[tap], NT, preferred_element_type=F32)
            o32[pl.ds(0, 256, stride=2), :] = both[:, 0:128]
            o32[pl.ds(1, 256, stride=2), :] = both[:, 128:256] + odd
            for row in range(4):
                gin[px, 8 * c + 2 * row + py] = o32[row * 128 : row * 128 + 128].astype(BF)
            return carry

        lax.fori_loop(begin, end, chunk, 0)

    def pack(first, slot, count=9):
        def step(i, carry):
            for side in range(4):
                found = q[first + i, pl.ds(side * 2 + 1 - core, 32, stride=8), :]
                pair_out[slot + i, side] = found.astype(BF).reshape(4, 8, 128)
            return carry

        lax.fori_loop(0, count, step, 0)

    def pair_copy(part, slot, count):
        at = pl.ds(slot, count)
        return remote(
            pair_out.at[at], pair_in.at[at], rs_send.at[part], rs_recv.at[part], (slab, grp + 1 - 2 * core)
        )

    def held(tap, slot, side):
        found = q[tap, pl.ds(side * 2 + core, 32, stride=8), :].reshape(4, 8, 128)
        return found + pair_in[slot, side].astype(F32)

    def ax_copy(part, d):
        to, i, at = (x + d) % 4, 4 + part * 3 + d, pl.ds(part * 9, 9)
        return remote(ax.at[to, at], ax_in.at[d - 1, at], rs_send.at[i], rs_recv.at[i], device(to, y, z, core))

    def ay_copy(part, d):
        to, i, at = (y + d) % 4, 10 + part * 18 + d, pl.ds(part * 9, 9)
        return remote(ay.at[to, at], ay_in.at[d - 1, at], rs_send.at[i], rs_recv.at[i], device(x, to, z, core))

    def by_copy(d):
        to_x, to_y, i = (x + d // 4) % 4, (y + d % 4) % 4, 13 + d
        return remote(
            by.at[to_x * 4 + to_y], by_in.at[d - 1], rs_send.at[i], rs_recv.at[i], device(to_x, to_y, z, core)
        )

    def add_x(slot, carry):
        found = ax[x, slot].astype(F32)
        for d in range(3):
            found = found + ax_in[d, slot].astype(F32)
        ay_own[slot] = found
        for block in range(4):
            ay[block, slot] = found[block].astype(BF)
        return carry

    def split_x(part):
        def step(i, carry):
            slot = part * 9 + i
            for side in range(4):
                found = held(9 + slot, slot, side).astype(BF)
                for block in range(4):
                    ax[block, slot, side] = found[block]
            return carry

        lax.fori_loop(0, 9, step, 0)

    join(a2_in, g_own)
    tap_grads(1, g_own, 0)
    pack(9, 0)
    pair_copy(0, 0, 9).start()
    tap_grads(2, g_own, 1)
    pack(18, 9)
    pair_copy(1, 9, 9).start()

    def first_wave(part):
        pair_copy(part, part * 9, 9).wait()
        split_x(part)
        for d in (1, 2, 3):
            ax_copy(part, d).start()

    def second_wave(part):
        for d in (1, 2, 3):
            ax_copy(part, d).wait()
        lax.fori_loop(part * 9, part * 9 + 9, add_x, 0)
        for d in (1, 2, 3):
            ay_copy(part, d).start()

    first_wave(0)
    turn(g_own, 0)
    edge_row(0).start()
    first_wave(1)
    finish_edge(0)
    second_wave(0)

    def on_wait(d, carry):
        on_copy(d).wait()
        return carry

    lax.fori_loop(0, 64, on_wait, 0)
    join(h_in, g_next, slab != 63)
    for ky in range(3):
        tap_grads(0, g_next, 1, (ky,))
        pack(3 * ky, 18 + 3 * ky, 3)
        pair_copy(2 + ky, 18 + 3 * ky, 3).start()
    turn(g_next, 1)
    edge_row(1).start()

    def split_y(i, carry):
        for side in range(4):
            found = held(i, 18 + i, side).astype(BF)
            for block in range(4):
                by[block * 4 + side, i] = found[block]
        return carry

    for ky in range(3):
        pair_copy(2 + ky, 18 + 3 * ky, 3).wait()
        lax.fori_loop(3 * ky, 3 * ky + 3, split_y, 0)
    for d in range(1, 16):
        by_copy(d).start()
    second_wave(1)
    finish_edge(1)
    input_grad(0, 0)
    input_grad(0, 1)
    input_grad(1, 0)
    for part in range(2):
        for d in (1, 2, 3):
            ay_copy(part, d).wait()
    for d in range(1, 16):
        by_copy(d).wait()
    own = x * 4 + y
    for tap in range(27):
        if tap < 9:
            found = by[own, tap].astype(F32)
            for d in range(15):
                found = found + by_in[d, tap].astype(F32)
        else:
            t = tap - 9
            found = ay_own[t, y]
            for d in range(3):
                found = found + ay_in[d, t].astype(F32)
        zz[tap * 8 : tap * 8 + 8, :] = found
    for row in range(8):
        zs[row] = zz[pl.ds(row, 27, stride=8), :].astype(BF)
    def z_copy(d):
        to, i = (z + d) % 8, 31 + d
        return remote(zs.at[to], zs_in.at[d - 1], rs_send.at[i], rs_recv.at[i], device(x, y, to, core))

    for d in range(1, 8):
        z_copy(d).start()
    input_grad(1, 1)
    for d in range(1, 8):
        z_copy(d).wait()
    found = zz[pl.ds(z, 27, stride=8), :]
    for d in range(7):
        found = found + zs_in[d].astype(F32)
    for tap in range(27):
        down_ref[tap] = found[tap : tap + 1] * scale


def write(gin, down, stat, gin_out, down_out, gain_out, shift_out, sem):
    copies = [
        pltpu.make_async_copy(gin, gin_out, sem.at[0]),
        pltpu.make_async_copy(down, down_out, sem.at[1]),
    ]
    for copy in copies:
        copy.start()
    row = lax.broadcasted_iota(jnp.int32, (8, 128), 0)
    lane = lax.broadcasted_iota(jnp.int32, (8, 128), 1)
    for ch in range(4):
        here = (row == ch) & (lane == 0)
        gain_out[ch] = jnp.sum(jnp.where(here, stat[0], 0.0))
        shift_out[ch] = jnp.sum(jnp.where(here, stat[1], 0.0))
    for copy in copies:
        copy.wait()


def local(fine_input, out_grad, pre_norm, act_out, norm_gain, w_down, w_up):
    cells = pre_norm.shape[1] * pre_norm.shape[2] * lax.axis_size("grp")
    arrays = (fine_input, out_grad, pre_norm, act_out, norm_gain, w_down, w_up)
    vmem = pl.BlockSpec(memory_space=pltpu.VMEM)
    smem = pl.BlockSpec(memory_space=pltpu.SMEM)
    hbm = pl.BlockSpec(memory_space=pltpu.HBM)
    dma = pltpu.SemaphoreType.DMA
    grad_input, down, stat = pl.pallas_call(
        functools.partial(kernel, float(cells), 1.0 / math.sqrt(cells)),
        out_shape=(
            jax.ShapeDtypeStruct((2, 32, 128, 128), BF),
            jax.ShapeDtypeStruct((27, 1, 128), F32),
            jax.ShapeDtypeStruct((2, 8, 128), F32),
        ),
        in_specs=[hbm] * 7,
        out_specs=(vmem, vmem, vmem),
        scratch_shapes=[
            pltpu.VMEM((2, 32, 128, 128), BF),
            pltpu.VMEM((2, 32, 128, 128), BF),
            pltpu.VMEM((4, 64, 1024), BF),
            pltpu.VMEM((4, 64, 1024), BF),
            pltpu.VMEM((27, 128, 256), BF),
            pltpu.VMEM((8, 256, 128), BF),
            pltpu.SMEM((4,), F32),
            pltpu.VMEM((4, 128, 128), F32),
            pltpu.VMEM((4, 256, 256), BF),
            pltpu.VMEM((256, 1024), F32),
            pltpu.VMEM((4, 1024, 256), BF),
            pltpu.VMEM((64, 8, 512), BF),
            pltpu.VMEM((64, 8, 512), BF),
            pltpu.VMEM((64, 8, 512), BF),
            pltpu.VMEM((64, 8, 512), BF),
            pltpu.VMEM((64, 8, 512), BF),
            pltpu.VMEM((4, 512, 128), F32),
            pltpu.VMEM((4, 512, 128), F32),
            pltpu.VMEM((4, 2, 8, 128), F32),
            pltpu.VMEM((4, 2, 8, 128), F32),
            pltpu.VMEM((2, 128, 128), BF),
            pltpu.VMEM((2, 1024, 384), BF),
            pltpu.VMEM((2, 1088, 384), BF),
            pltpu.VMEM((256, 1024), BF),
            pltpu.VMEM((256, 1024), BF),
            pltpu.VMEM((2, 1088, 256), BF),
            pltpu.VMEM((2, 1088, 256), BF),
            pltpu.VMEM((27, 256, 128), F32),
            pltpu.VMEM((512, 128), F32),
            pltpu.VMEM((27, 4, 4, 8, 128), BF),
            pltpu.VMEM((27, 4, 4, 8, 128), BF),
            pltpu.VMEM((4, 18, 4, 8, 128), BF),
            pltpu.VMEM((3, 18, 4, 8, 128), BF),
            pltpu.VMEM((16, 9, 8, 128), BF),
            pltpu.VMEM((15, 9, 8, 128), BF),
            pltpu.VMEM((4, 18, 8, 128), BF),
            pltpu.VMEM((3, 18, 8, 128), BF),
            pltpu.VMEM((18, 4, 8, 128), F32),
            pltpu.VMEM((216, 128), F32),
            pltpu.VMEM((8, 27, 128), BF),
            pltpu.VMEM((7, 27, 128), BF),
            dma((7,)),
            dma((64,)), dma((64,)), dma((64,)), dma((64,)), dma((64,)), dma((64,)),
            dma((4,)), dma((4,)), dma((4,)), dma((4,)),
            dma((3,)), dma((3,)), dma((40,)), dma((40,)),
        ],
        compiler_params=pltpu.CompilerParams(
            collective_id=0, has_side_effects=True, vmem_limit_bytes=40 * 1024 * 1024
        ),
    )(*[pltpu.with_memory_space_constraint(array, pltpu.HBM) for array in arrays])
    grad_input, down, gain, shift = pl.pallas_call(
        write,
        out_shape=(
            jax.ShapeDtypeStruct((2, 32, 128, 128), BF),
            jax.ShapeDtypeStruct((27, 1, 128), F32),
            jax.ShapeDtypeStruct((4,), F32),
            jax.ShapeDtypeStruct((4,), F32),
        ),
        in_specs=[vmem] * 3,
        out_specs=(hbm, hbm, smem, smem),
        scratch_shapes=[dma((2,))],
        compiler_params=pltpu.CompilerParams(vmem_limit_bytes=2 * 1024 * 1024),
    )(grad_input, down, stat)
    return (grad_input, down.transpose(1, 0, 2), gain, shift)


def solution(mesh):
    return jax.shard_map(
        local,
        mesh=mesh,
        in_specs=(
            P("slab", "grp", None, None),
            P("slab", "grp", None, None),
            P("slab", None, "grp"),
            P("slab", None, "grp"),
            P("slab"),
            P(),
            P(),
        ),
        out_specs=(
            P("slab", "grp", None, None),
            P(("slab", "grp"), None, None),
            P("slab"),
            P("slab"),
        ),
        check_vma=False,
    )
```
